32 devices in a mesh: frame: 2 (over y), plane: 16 (over z, x, core).
Axes of the slice: x: 2, y: 2, z: 4, core: 2. Of those that a mesh axis runs over, the one named last changes fastest.
Arguments:
- states: float32 [4, 2, 16, 256, 256], P(None, 'frame', 'plane'), may hold values from -6 to 6
- measured: float32 [2, 16, 256, 256], P('frame', 'plane'), may hold values from -6 to 6
- response: float32 [256, 256], replicated, may hold values from 0.1 to 10
- kernel_in: bfloat16 [3, 9, 32, 2], replicated, may hold values from -1.5 to 1.5
- bias_in: float32 [3, 32], replicated, may hold values from -3 to 3
- kernel_mid: bfloat16 [3, 1, 9, 32, 32], replicated, may hold values from -0.375 to 0.375
- bias_mid: float32 [3, 1, 32], replicated, may hold values from -3 to 3
- kernel_out: bfloat16 [3, 9, 32], replicated, may hold values from -0.375 to 0.375
Outputs:
- new_states: float32 [4, 2, 16, 256, 256], P(None, 'frame', 'plane')
The draws below stay inside these ranges and needn't reach their ends.
All inputs are finite; a program needn't handle non-finite values.
Results may differ from the reference program's by a relative error of at most 0.0056.
Values may be sent and summed in bfloat16 or wider, within the bound.
No kernel may reach another device: no remote copies, remote signals or barrier semaphores. Data moves between devices by JAX's collectives and lax.ppermute only.
A program may use at most 192 MiB of HBM per device.

```python
import math
import jax
import jax.numpy as jnp
from jax import lax

N = 256
C = 32
LAYERS = 3
Z = 16


def levels(stream_key, dims, shards, low, top_value):
    def one(axis_at, parts):
        heights = jax.random.uniform(jax.random.fold_in(jax.random.fold_in(stream_key, 6), axis_at), (parts,), jnp.float32, low / len(shards), top_value / len(shards))
        return jnp.repeat(jnp.exp(heights), dims[axis_at] // parts).reshape((-1,) + (1,) * (len(dims) - axis_at - 1))

    loudness = one(*shards[0])
    for cut in shards[1:]:
        loudness = loudness * one(*cut)
    return loudness


def centred(stream_key, shape, scale, reach, shards=(), kind=jnp.bfloat16):
    drawn = scale * jax.random.normal(stream_key, shape, jnp.float32)
    if shards:
        drawn = drawn * levels(stream_key, shape, shards, -0.22, 0.18)
    return jnp.clip(drawn, -reach, reach).astype(kind)


def setup_inputs(seed: int = 0) -> dict:
    seeds = jax.random.split(jax.random.key(seed), 9)
    return {
        "states": centred(seeds[0], (4, 2, Z, N, N), 1.0, 6.0, ((1, 2), (2, 16)), jnp.float32),
        "measured": centred(seeds[1], (2, Z, N, N), 1.0, 6.0, ((0, 2), (1, 16)), jnp.float32),
        "response": jnp.clip(jnp.exp(jax.random.uniform(seeds[2], (N, N), jnp.float32, math.log(0.1), math.log(10.0))), 0.1, 10.0),
        "kernel_in": centred(seeds[3], (3, 9, C, 2), 18 ** -0.5, 1.5),
        "bias_in": centred(seeds[4], (3, C), 0.5, 3.0, (), jnp.float32),
        "kernel_mid": centred(seeds[5], (3, LAYERS - 2, 9, C, C), (9 * C) ** -0.5, 0.375),
        "bias_mid": centred(seeds[6], (3, LAYERS - 2, C), 0.5, 3.0, (), jnp.float32),
        "kernel_out": centred(seeds[7], (3, 9, C), (9 * C) ** -0.5, 0.375),
    }


relaxation = 0.8


def fourier_tables(length):
    indices = jnp.arange(length, dtype=jnp.int32)
    phase = (indices[:, None] * indices[None, :]) % length
    angle = phase.astype(jnp.float32) * (2.0 * math.pi / length)
    return jnp.cos(angle).astype(jnp.bfloat16), jnp.sin(angle).astype(jnp.bfloat16)


def along_last(values, table):
    return jnp.einsum("pyx,kx->pyk", values.astype(jnp.float32), table.astype(jnp.float32), precision=lax.Precision.HIGHEST)


def along_middle(table, values):
    return jnp.einsum("ky,pyx->pkx", table.astype(jnp.float32), values.astype(jnp.float32), precision=lax.Precision.HIGHEST)


def fidelity(volume, filter_gain):
    length = volume.shape[2]
    cosine, sines = fourier_tables(length)
    source = volume.astype(jnp.bfloat16)
    row_real = along_last(source, cosine).astype(jnp.bfloat16)
    row_imag = (-along_last(source, sines)).astype(jnp.bfloat16)
    spec_real = ((along_middle(cosine, row_real) + along_middle(sines, row_imag)) * filter_gain).astype(jnp.bfloat16)
    spec_imag = ((along_middle(cosine, row_imag) - along_middle(sines, row_real)) * filter_gain).astype(jnp.bfloat16)
    back_real = (along_middle(cosine, spec_real) - along_middle(sines, spec_imag)).astype(jnp.bfloat16)
    back_imag = (along_middle(cosine, spec_imag) + along_middle(sines, spec_real)).astype(jnp.bfloat16)
    spatial = along_last(back_real, cosine) - along_last(back_imag, sines)
    return spatial * (1.0 / (length * length))


def convolve(planes_in, kernel):
    rows_count = planes_in.shape[1]
    cols_count = planes_in.shape[2]
    padded = jnp.pad(planes_in, ((0, 0), (1, 1), (1, 1))).astype(jnp.float32)
    summed = jnp.zeros((kernel.shape[1], rows_count, cols_count), jnp.float32)
    for tap_index in range(9):
        row_shift = tap_index // 3
        col_shift = tap_index % 3
        shifted = padded[:, row_shift:row_shift + rows_count, col_shift:col_shift + cols_count]
        summed = summed + jnp.einsum("oc,cab->oab", kernel[tap_index].astype(jnp.float32), shifted)
    return summed


def denoise(channels, which, kernel_in, bias_in, kernel_mid, bias_mid, kernel_out):
    def single_plane(planes_in):
        hidden = jax.nn.relu(convolve(planes_in, kernel_in[which]) + bias_in[which][:, None, None]).astype(jnp.bfloat16)
        for section in range(kernel_mid.shape[1]):
            hidden = jax.nn.relu(convolve(hidden, kernel_mid[which, section]) + bias_mid[which, section][:, None, None]).astype(jnp.bfloat16)
        return convolve(hidden, kernel_out[which][:, None, :])[0].astype(jnp.bfloat16)
    return lax.map(single_plane, channels)


def reference(states, measured, response, kernel_in, bias_in, kernel_mid, bias_mid, kernel_out):
    filter_gain = 1.0 / (1.0 + response)
    rounded = states.astype(jnp.bfloat16)
    results = []
    for frame_index in range(2):
        other = 1 - frame_index
        current = states[:, frame_index]
        data_estimate = fidelity(measured[frame_index] + current[0], filter_gain)
        channels_z = jnp.stack([rounded[1, frame_index], rounded[1, other]], 1)
        residual_z = denoise(channels_z, 0, kernel_in, bias_in, kernel_mid, bias_mid, kernel_out)
        channels_x = jnp.stack([jnp.transpose(rounded[2, frame_index], (2, 0, 1)), jnp.transpose(rounded[2, other], (2, 0, 1))], 1)
        residual_x = jnp.transpose(denoise(channels_x, 1, kernel_in, bias_in, kernel_mid, bias_mid, kernel_out), (1, 2, 0))
        channels_y = jnp.stack([jnp.transpose(rounded[3, frame_index], (1, 0, 2)), jnp.transpose(rounded[3, other], (1, 0, 2))], 1)
        residual_y = jnp.transpose(denoise(channels_y, 2, kernel_in, bias_in, kernel_mid, bias_mid, kernel_out), (1, 0, 2))
        estimates = jnp.stack([
            data_estimate,
            current[1] - residual_z.astype(jnp.float32),
            current[2] - residual_x.astype(jnp.float32),
            current[3] - residual_y.astype(jnp.float32)])
        reflected = 2.0 * estimates - current
        average = jnp.mean(reflected, axis=0)
        results.append((1.0 - relaxation) * current + relaxation * (2.0 * average - reflected))
    return jnp.stack(results, 1)
```

```python
import functools
import math

import jax
import jax.numpy as jnp
import numpy as np
from jax import lax
from jax.experimental import pallas as pl
from jax.experimental.pallas import tpu as pltpu
from jax.sharding import PartitionSpec as P

relaxation = 0.8

BF = jnp.bfloat16
F32 = jnp.float32

CHUNK = 16
WINDOW = 32
LEAD = 8

FIRST_TAP = {(0, 3): 0, (0, 0): 1, (0, 1): 2, (1, 0): 0, (1, 1): 1, (1, 2): 2}
LATER_TAP = {
    (0, 0, 0): 1, (0, 0, 1): 2, (1, 0, 1): 0,
    (0, 1, 0): 0, (0, 1, 1): 1, (1, 1, 0): 2,
}


def fourier_tables(length):
    indices = np.arange(length, dtype=np.int64)
    phase = indices[:, None] * indices[None, :] % length
    angle = phase.astype(np.float32) * np.float32(2.0 * math.pi / length)
    return np.cos(angle).astype(BF), np.sin(angle).astype(BF)


def mm(a, b):
    return jnp.dot(a, b, preferred_element_type=F32)


def nt(a, b):
    return lax.dot_general(a, b, (((1,), (1,)), ((), ())), preferred_element_type=F32)


def tn(a, b):
    return lax.dot_general(a, b, (((0,), (0,)), ((), ())), preferred_element_type=F32)


def iota(shape, axis):
    return lax.broadcasted_iota(jnp.int32, shape, axis)


def parity_matrix(n):
    half = n // 2
    row, col = iota((n, n), 0), iota((n, n), 1)
    natural = jnp.where(col < half, 2 * col, 2 * (col - half) + 1)
    return (row == natural).astype(F32).astype(BF)


def whole(shape):
    zeros = (0,) * len(shape)
    return pl.BlockSpec(shape, lambda i: zeros)


def agent(k, n):
    return pl.BlockSpec((1, n, n), lambda i: (k, 0, 0))


def cost(flops, moved):
    return pl.CostEstimate(flops=flops, bytes_accessed=moved, transcendentals=0)


def spread_kernel(devices, fast, w1, w2, w3, z_ref, *outs):
    n = w1.shape[1]
    split = parity_matrix(n)
    z_ref[...] = mm(w1[0].astype(BF), split).astype(BF)
    toward_x = tn(w2[0].astype(BF), split)
    toward_y = mm(w3[0].astype(BF), split)
    if fast:
        per = n // devices
        both = jnp.concatenate(
            [toward_x.reshape(devices, per, n), toward_y.reshape(devices, per, n)], 1
        )
        outs[0][...] = both.reshape(2 * n, n).astype(BF)
    else:
        outs[0][...] = toward_x.astype(BF)
        outs[1][...] = toward_y.astype(BF)


def spread(current, devices):
    n = current.shape[1]
    per = n // devices
    fast = per % 8 == 0
    plane = jax.ShapeDtypeStruct((n, n), BF)
    shapes = [plane, jax.ShapeDtypeStruct((2 * n, n), BF)] if fast else [plane] * 3
    outs = pl.pallas_call(
        functools.partial(spread_kernel, devices, fast),
        out_shape=shapes,
        grid=(1,),
        in_specs=[agent(1, n), agent(2, n), agent(3, n)],
        out_specs=[whole(s.shape) for s in shapes],
        cost_estimate=cost(6 * n**3, 18 * n * n),
        name="spread",
    )(current, current, current)
    if fast:
        return outs[0], outs[1]
    parts = [o.reshape(devices, per, n) for o in outs[1:]]
    return outs[0], jnp.concatenate(parts, 1).reshape(2 * n, n)


def build_first(taps, channels):
    wide = 8 * WINDOW
    lane = iota((channels, wide), 1)
    at_row = lane % WINDOW
    pick_row = iota((6, wide), 0)
    pick_lane = iota((6, wide), 1) // WINDOW
    vectors = {}
    for parity in range(2):
        pick = jnp.zeros((6, wide), F32)
        for group in range(4):
            tap = FIRST_TAP.get((parity, group))
            if tap is not None:
                for source in range(2):
                    hit = (pick_row == 2 * tap + source) & (pick_lane == 4 * source + group)
                    pick = jnp.where(hit, 1.0, pick)
        pick = pick.astype(BF)
        for p in range(3):
            vectors[parity, p] = mm(taps[p], pick)
    pieces = []
    for row in range(CHUNK):
        for parity in range(2):
            piece = jnp.zeros((channels, wide), F32)
            for p in range(3):
                piece = jnp.where(at_row == row + LEAD - 1 + p, vectors[parity, p], piece)
            pieces.append(piece.astype(BF))
    return pieces


def build_mid(taps, channels):
    wide = 8 * channels
    block = iota((channels, wide), 1) // channels
    repeat = (iota((channels, wide), 0) == iota((channels, wide), 1) % channels).astype(F32).astype(BF)
    spread_taps = mm(taps, repeat)
    pieces = []
    for shifted in range(2):
        for row in range(2):
            for parity in range(2):
                piece = jnp.zeros((channels, wide), F32)
                for p in range(3):
                    for source in range(2):
                        tap = LATER_TAP.get((shifted, parity, source))
                        if tap is not None:
                            t = 3 * p + tap
                            value = spread_taps[t * channels : (t + 1) * channels]
                            piece = jnp.where(block == 2 * (row + p) + source, value, piece)
                pieces.append(piece.astype(BF))
    return pieces


def build_last(taps, channels):
    wide = (CHUNK + 2) * 2 * channels
    lane = iota((channels, wide), 1)
    at_row = iota((CHUNK, wide), 1) // (2 * channels)
    out_row = iota((CHUNK, wide), 0)
    spread_taps = []
    for source in range(2):
        hit = (lane % channels == iota((channels, wide), 0)) & (lane // channels % 2 == source)
        spread_taps.append(mm(taps, hit.astype(F32).astype(BF)))
    pieces = []
    for shifted in range(2):
        for parity in range(2):
            piece = jnp.zeros((CHUNK, wide), F32)
            for p in range(3):
                value = jnp.zeros((1, wide), F32)
                for source in range(2):
                    tap = LATER_TAP.get((shifted, parity, source))
                    if tap is not None:
                        t = 3 * p + tap
                        value = value + spread_taps[source][t : t + 1]
                piece = jnp.where(at_row == out_row + p, value, piece)
            pieces.append(piece.astype(BF))
    return pieces


def column(row_vector, lanes):
    size = row_vector.shape[1]
    square = iota((size, size), 0) == iota((size, size), 1)
    spread_rows = jnp.where(square, jnp.broadcast_to(row_vector, (size, size)), 0.0)
    return jnp.broadcast_to(jnp.sum(spread_rows, 1, keepdims=True), (size, lanes))


def prepare_kernel(
    w0, measured, response, cos_ref, sin_ref, kin, bin_, kmid, bmid, kout,
    data_ref, first_ref, mid_ref, last_ref, bias_ref,
):
    n = response.shape[0]
    channels = kmid.shape[2]
    lanes = bias_ref.shape[3]
    cosine, sines = cos_ref[...], sin_ref[...]
    gain = 1.0 / (1.0 + response[...])
    source = (measured[0] + w0[0]).astype(BF)
    row_real = mm(source, cosine).astype(BF)
    row_imag = (-mm(source, sines)).astype(BF)
    spec_real = ((mm(cosine, row_real) + mm(sines, row_imag)) * gain).astype(BF)
    spec_imag = ((mm(cosine, row_imag) - mm(sines, row_real)) * gain).astype(BF)
    back_real = (mm(cosine, spec_real) - mm(sines, spec_imag)).astype(BF)
    back_imag = (mm(cosine, spec_imag) + mm(sines, spec_real)).astype(BF)
    data_ref[...] = (mm(back_real, cosine) - mm(back_imag, sines)) * (1.0 / (n * n))
    for which in range(3):
        for index, piece in enumerate(build_first([kin[which, p] for p in range(3)], channels)):
            first_ref[which, pl.ds(index * channels, channels), :] = piece
        for index, piece in enumerate(build_mid(kmid[which], channels)):
            mid_ref[which, pl.ds(index * channels, channels), :] = piece
        for index, piece in enumerate(build_last(kout[which], channels)):
            last_ref[which, pl.ds(index * CHUNK, CHUNK), :] = piece
        bias_ref[which, 0] = column(bin_[pl.ds(which, 1), :], lanes)
        bias_ref[which, 1] = column(bmid[pl.ds(which, 1), :], lanes)


def prepare(current, measured, response, kernel_in, bias_in, kernel_mid, bias_mid, kernel_out):
    n = response.shape[0]
    channels = bias_in.shape[1]
    lanes = n // 2
    cosine, sines = fourier_tables(n)
    kin = kernel_in.reshape(3, 3, 3, channels, 2).transpose(0, 1, 3, 2, 4).reshape(3, 3, channels, 6)
    kmid = kernel_mid[:, 0].reshape(3, 9 * channels, channels)
    bmid = bias_mid[:, 0]
    wide = (CHUNK + 2) * 2 * channels
    shapes = [
        jax.ShapeDtypeStruct((n, n), F32),
        jax.ShapeDtypeStruct((3, CHUNK * 2 * channels, 8 * WINDOW), BF),
        jax.ShapeDtypeStruct((3, 8 * channels, 8 * channels), BF),
        jax.ShapeDtypeStruct((3, 4 * CHUNK, wide), BF),
        jax.ShapeDtypeStruct((3, 2, channels, lanes), F32),
    ]
    args = [response, jnp.asarray(cosine), jnp.asarray(sines), kin, bias_in, kmid, bmid, kernel_out]
    return pl.pallas_call(
        prepare_kernel,
        out_shape=shapes,
        grid=(1,),
        in_specs=[agent(0, n), agent(0, n)] + [whole(a.shape) for a in args],
        out_specs=[whole(s.shape) for s in shapes],
        cost_estimate=cost(40 * n**3, 40 * n * n),
        name="prepare",
    )(current, measured, *args)


def shifted_columns(values, parity, lanes):
    lane = iota((values.shape[0], lanes), 1)
    pieces = []
    for start in range(0, values.shape[1], lanes):
        part = values[:, start : start + lanes]
        if parity == 0:
            part = jnp.where(lane == 0, 0.0, pltpu.roll(part, 1, 1))
        else:
            part = jnp.where(lane == lanes - 1, 0.0, pltpu.roll(part, lanes - 1, 1))
        pieces.append(part)
    return jnp.concatenate(pieces, 1) if len(pieces) > 1 else pieces[0]


def halve(value):
    return jnp.maximum(value.astype(BF), jnp.zeros((), BF))


def first_layer(window, weights, bias, hidden_ref, base, channels):
    step = 8 * channels
    for index in range(CHUNK * 2 * channels // step):
        product = mm(weights[pl.ds(index * step, step), :], window)
        for part in range(step // channels):
            piece = product[part * channels : (part + 1) * channels] + bias
            hidden_ref[pl.ds(base + index * step + part * channels, channels), :] = halve(piece)


def mid_layer(slab, weights, bias, out_ref, base, channels, lanes):
    product = mm(weights, slab)
    for part in range(4):
        kept = product[part * channels : (part + 1) * channels]
        moved = product[(4 + part) * channels : (5 + part) * channels]
        piece = kept + shifted_columns(moved, part % 2, lanes) + bias
        out_ref[pl.ds(base + part * channels, channels), :] = halve(piece)


def last_layer(slab, weights, lanes):
    product = mm(weights, slab)
    return [
        product[parity * CHUNK : (parity + 1) * CHUNK]
        + shifted_columns(product[(2 + parity) * CHUNK : (3 + parity) * CHUNK], parity, lanes)
        for parity in range(2)
    ]


def planes_kernel(
    frames, depth, per, channels,
    arrived_ref, first_ref, mid_ref, last_ref, bias_ref, out_ref,
    source, result, window, hidden, deeper,
):
    lanes = arrived_ref.shape[1] // 2
    stride = 2 * per
    row = 2 * channels
    for half in range(2):
        source[half] = arrived_ref[:, half * lanes : (half + 1) * lanes].astype(F32)
    window[...] = jnp.zeros_like(window)
    for ref in (hidden, deeper):
        ref[0:row, :] = jnp.zeros((row, frames * lanes), BF)
        ref[pl.ds(row * (depth + 1), row), :] = jnp.zeros((row, frames * lanes), BF)

    def pair(step, _):
        which = step // per + 1
        for frame in range(frames):
            base = frame * depth * stride + step
            even = source[0, pl.ds(base, depth, stride), :]
            odd = source[1, pl.ds(base, depth, stride), :]
            groups = [even, odd, shifted_columns(even, 1, lanes), shifted_columns(odd, 0, lanes)]
            for image in range(frames):
                channel = (frame - image) % frames
                for group in range(4):
                    window[4 * channel + group, pl.ds(LEAD, depth), pl.ds(image * lanes, lanes)] = groups[group]
        bias1 = jnp.concatenate([bias_ref[which, 0]] * frames, 1)
        bias2 = jnp.concatenate([bias_ref[which, 1]] * frames, 1)
        for chunk in range(depth // CHUNK):
            rows = window[:, pl.ds(chunk * CHUNK, WINDOW), :]
            rows = rows.astype(BF).reshape(8 * WINDOW, frames * lanes)
            first_layer(rows, first_ref.at[which], bias1, hidden, row * (1 + chunk * CHUNK), channels)
        for strip in range(depth // 2):
            slab = hidden[pl.ds(2 * row * strip, 4 * row), :]
            mid_layer(slab, mid_ref[which], bias2, deeper, row * (1 + 2 * strip), channels, lanes)
        for chunk in range(depth // CHUNK):
            slab = deeper[pl.ds(chunk * CHUNK * row, (CHUNK + 2) * row), :]
            parts = last_layer(slab, last_ref[which], lanes)
            for half in range(2):
                for frame in range(frames):
                    base = (frame * depth + chunk * CHUNK) * stride + step
                    result[half, pl.ds(base, CHUNK, stride), :] = parts[half][:, frame * lanes : (frame + 1) * lanes]
        return 0

    lax.fori_loop(0, 2 * per, pair, 0)
    for half in range(2):
        out_ref[:, half * lanes : (half + 1) * lanes] = result[half].astype(BF)


def planes(arrived, first, mid, last, bias, frames, depth):
    rows, n = arrived.shape
    lanes = n // 2
    channels = bias.shape[2]
    per = n // (frames * depth)
    row = 2 * channels
    args = [arrived, first, mid, last, bias]
    return pl.pallas_call(
        functools.partial(planes_kernel, frames, depth, per, channels),
        out_shape=jax.ShapeDtypeStruct((rows, n), BF),
        grid=(1,),
        in_specs=[whole(a.shape) for a in args],
        out_specs=whole((rows, n)),
        scratch_shapes=[
            pltpu.VMEM((2, rows, lanes), F32),
            pltpu.VMEM((2, rows, lanes), F32),
            pltpu.VMEM((8, depth + 2 * LEAD, frames * lanes), F32),
            pltpu.VMEM((row * (depth + 2), frames * lanes), BF),
            pltpu.VMEM((row * (depth + 2), frames * lanes), BF),
        ],
        cost_estimate=cost(2 * 9 * channels * channels * 2 * n * n * 3, 4 * n * n),
        name="planes",
    )(*args)


def volume_kernel(
    channels, mine_ref, other_ref, first_ref, mid_ref, last_ref, bias_ref, after_ref, out_ref,
    window, hidden, deeper,
):
    n = mine_ref.shape[0]
    lanes = n // 2
    row = 2 * channels
    depth = n // 2
    edge = row * (depth + 1)
    zeros = jnp.zeros((8, LEAD, lanes), F32)
    window[:, 0:LEAD, :] = zeros
    window[:, pl.ds(LEAD + n, LEAD), :] = zeros
    for channel, ref in enumerate((mine_ref, other_ref)):
        even = ref[:, :lanes].astype(F32)
        odd = ref[:, lanes:].astype(F32)
        groups = [even, odd, shifted_columns(even, 1, lanes), shifted_columns(odd, 0, lanes)]
        for group in range(4):
            window[4 * channel + group, pl.ds(LEAD, n), :] = groups[group]
    bias1 = jnp.concatenate([bias_ref[0, 0]] * 2, 1)
    bias2 = jnp.concatenate([bias_ref[0, 1]] * 2, 1)

    def seam(ref):
        ref[0:row, 0:lanes] = jnp.zeros((row, lanes), BF)
        ref[pl.ds(edge, row), pl.ds(lanes, lanes)] = jnp.zeros((row, lanes), BF)
        ref[0:row, pl.ds(lanes, lanes)] = ref[pl.ds(edge - row, row), 0:lanes]
        ref[pl.ds(edge, row), 0:lanes] = ref[row : 2 * row, pl.ds(lanes, lanes)]

    def first_step(chunk, _):
        halves = [
            window[:, pl.ds(pl.multiple_of(side * depth + chunk * CHUNK, 8), WINDOW), :] for side in range(2)
        ]
        rows = jnp.concatenate(halves, 2).astype(BF).reshape(8 * WINDOW, 2 * lanes)
        base = pl.multiple_of(row * (1 + chunk * CHUNK), row)
        first_layer(rows, first_ref.at[0], bias1, hidden, base, channels)
        return 0

    lax.fori_loop(0, depth // CHUNK, first_step, 0)
    seam(hidden)

    def mid_step(step, _):
        for inner in range(4):
            strip = step * 4 + inner
            slab = hidden[pl.ds(pl.multiple_of(2 * row * strip, row), 4 * row), :]
            base = pl.multiple_of(row * (1 + 2 * strip), row)
            mid_layer(slab, mid_ref[0], bias2, deeper, base, channels, lanes)
        return 0

    lax.fori_loop(0, depth // 8, mid_step, 0)
    seam(deeper)

    def last_step(chunk, _):
        slab = deeper[pl.ds(pl.multiple_of(chunk * CHUNK * row, row), (CHUNK + 2) * row), :]
        parts = last_layer(slab, last_ref[0], lanes)
        for half in range(2):
            for side in range(2):
                base = pl.multiple_of(side * depth + chunk * CHUNK, CHUNK)
                piece = parts[half][:, side * lanes : (side + 1) * lanes]
                out_ref[pl.ds(base, CHUNK), pl.ds(half * lanes, lanes)] = piece.astype(BF)
        return 0

    lax.fori_loop(0, depth // CHUNK, last_step, 0)


def volume(mine, other, first, mid, last, bias, after):
    n = mine.shape[0]
    lanes = n // 2
    channels = bias.shape[2]
    row = 2 * channels
    args = [mine, other]
    tables = [first, mid, last, bias]
    return pl.pallas_call(
        functools.partial(volume_kernel, channels),
        out_shape=jax.ShapeDtypeStruct((n, n), BF),
        grid=(1,),
        in_specs=[whole(a.shape) for a in args]
        + [whole((1,) + t.shape[1:]) for t in tables]
        + [pl.BlockSpec(memory_space=pl.ANY)],
        out_specs=whole((n, n)),
        scratch_shapes=[
            pltpu.VMEM((8, n + 2 * LEAD, lanes), F32),
            pltpu.VMEM((row * (n // 2 + 2), n), BF),
            pltpu.VMEM((row * (n // 2 + 2), n), BF),
        ],
        cost_estimate=cost(2 * 9 * channels * channels * n * n * 3, 4 * n * n),
        name="volume",
    )(*args, *tables, after)


def combine_kernel(devices, fast, states, data, res_z, *refs):
    n = data.shape[0]
    out = refs[-1]
    split = parity_matrix(n)
    if fast:
        per = n // devices
        both = refs[0][...].astype(F32).reshape(devices, 2 * per, n)
        by_x = both[:, :per].reshape(n, n).astype(BF)
        by_y = both[:, per:].reshape(n, n).astype(BF)
    else:
        by_x, by_y = refs[0][...], refs[1][...]
    residuals = [nt(res_z[...], split), nt(split, by_x), nt(by_y, split)]
    current = [states[k] for k in range(4)]
    estimates = [data[...]] + [current[k + 1] - residuals[k] for k in range(3)]
    reflected = [2.0 * estimates[k] - current[k] for k in range(4)]
    average = (reflected[0] + reflected[1] + reflected[2] + reflected[3]) * 0.25
    for k in range(4):
        out[k] = (1.0 - relaxation) * current[k] + relaxation * (2.0 * average - reflected[k])


def combine(current, data, res_z, returned, devices):
    n = data.shape[0]
    per = n // devices
    fast = per % 8 == 0
    if fast:
        parts = [returned]
    else:
        shaped = returned.reshape(devices, 2, per, n)
        parts = [shaped[:, 0].reshape(n, n), shaped[:, 1].reshape(n, n)]
    args = [current, data, res_z] + parts
    return pl.pallas_call(
        functools.partial(combine_kernel, devices, fast),
        out_shape=jax.ShapeDtypeStruct(current.shape, F32),
        grid=(1,),
        in_specs=[whole(a.shape) for a in args],
        out_specs=whole(current.shape),
        cost_estimate=cost(6 * n**3, 40 * n * n),
        name="combine",
    )(*args)


def exchanged(rows, devices):
    n = rows.shape[1]
    blocks = rows.reshape(devices, rows.shape[0] // devices, n)
    blocks = lax.all_to_all(blocks, ("frame", "plane"), split_axis=0, concat_axis=0, tiled=True)
    return blocks.reshape(rows.shape)


def on_device(states, measured, response, kernel_in, bias_in, kernel_mid, bias_mid, kernel_out):
    frames = lax.axis_size("frame")
    depth = lax.axis_size("plane")
    devices = frames * depth
    current = states[:, 0, 0]
    mine, toward = spread(current, devices)
    other = lax.ppermute(mine, "frame", [(f, frames - 1 - f) for f in range(frames)])
    arrived = exchanged(toward, devices)
    data, first, mid, last, bias = prepare(
        current, measured[:, 0], response, kernel_in, bias_in, kernel_mid, bias_mid, kernel_out
    )
    residual = planes(arrived, first, mid, last, bias, frames, depth)
    returned = exchanged(residual, devices)
    res_z = volume(mine, other, first, mid, last, bias, residual)
    return combine(current, data, res_z, returned, devices)[:, None, None]


def solution(mesh):
    placed = (
        P(None, "frame", "plane", None, None),
        P("frame", "plane", None, None),
        P(),
        P(),
        P(),
        P(),
        P(),
        P(),
    )
    return jax.shard_map(
        on_device,
        mesh=mesh,
        in_specs=placed,
        out_specs=P(None, "frame", "plane", None, None),
        check_vma=False,
    )
```

```python
import functools
import math

import jax
import jax.numpy as jnp
import numpy as np
from jax import lax
from jax.experimental import pallas as pl
from jax.experimental.pallas import tpu as pltpu
from jax.sharding import PartitionSpec as P

relaxation = 0.8

BF = jnp.bfloat16
F32 = jnp.float32

CHUNK = 16
FIRST = 8
WINDOW = 16
LEAD = 4

FIRST_TAP = {(0, 3): 0, (0, 0): 1, (0, 1): 2, (1, 0): 0, (1, 1): 1, (1, 2): 2}
LATER_TAP = {
    (0, 0, 0): 1, (0, 0, 1): 2, (1, 0, 1): 0,
    (0, 1, 0): 0, (0, 1, 1): 1, (1, 1, 0): 2,
}


def fourier_tables(length):
    indices = np.arange(length, dtype=np.int64)
    phase = indices[:, None] * indices[None, :] % length
    angle = phase.astype(np.float32) * np.float32(2.0 * math.pi / length)
    return np.cos(angle).astype(BF), np.sin(angle).astype(BF)


def mm(a, b):
    return jnp.dot(a, b, preferred_element_type=F32)


def nt(a, b):
    return lax.dot_general(a, b, (((1,), (1,)), ((), ())), preferred_element_type=F32)


def tn(a, b):
    return lax.dot_general(a, b, (((0,), (0,)), ((), ())), preferred_element_type=F32)


def iota(shape, axis):
    return lax.broadcasted_iota(jnp.int32, shape, axis)


def parity_matrix(n):
    half = n // 2
    row, col = iota((n, n), 0), iota((n, n), 1)
    natural = jnp.where(col < half, 2 * col, 2 * (col - half) + 1)
    return (row == natural).astype(F32).astype(BF)


def whole(shape):
    zeros = (0,) * len(shape)
    return pl.BlockSpec(shape, lambda i: zeros)


def agent(k, n):
    return pl.BlockSpec((1, n, n), lambda i: (k, 0, 0))


def cost(flops, moved):
    return pl.CostEstimate(flops=flops, bytes_accessed=moved, transcendentals=0)


def spread_kernel(devices, fast, w1, w2, w3, z_ref, *outs):
    n = w1.shape[1]
    split = parity_matrix(n)
    z_ref[...] = mm(w1[0].astype(BF), split).astype(BF)
    toward_x = tn(w2[0].astype(BF), split)
    toward_y = mm(w3[0].astype(BF), split)
    if fast:
        per = n // devices
        both = jnp.concatenate(
            [toward_x.reshape(devices, per, n), toward_y.reshape(devices, per, n)], 1
        )
        outs[0][...] = both.reshape(2 * n, n).astype(BF)
    else:
        outs[0][...] = toward_x.astype(BF)
        outs[1][...] = toward_y.astype(BF)


def spread(current, devices):
    n = current.shape[1]
    per = n // devices
    fast = per % 8 == 0
    plane = jax.ShapeDtypeStruct((n, n), BF)
    shapes = [plane, jax.ShapeDtypeStruct((2 * n, n), BF)] if fast else [plane] * 3
    outs = pl.pallas_call(
        functools.partial(spread_kernel, devices, fast),
        out_shape=shapes,
        grid=(1,),
        in_specs=[agent(1, n), agent(2, n), agent(3, n)],
        out_specs=[whole(s.shape) for s in shapes],
        cost_estimate=cost(6 * n**3, 18 * n * n),
        name="spread",
    )(current, current, current)
    if fast:
        return outs[0], outs[1]
    parts = [o.reshape(devices, per, n) for o in outs[1:]]
    return outs[0], jnp.concatenate(parts, 1).reshape(2 * n, n)


def build_first(taps, channels):
    wide = 8 * WINDOW
    lane = iota((channels, wide), 1)
    at_row = lane % WINDOW
    pick_row = iota((6, wide), 0)
    pick_lane = iota((6, wide), 1) // WINDOW
    vectors = {}
    for parity in range(2):
        pick = jnp.zeros((6, wide), F32)
        for group in range(4):
            tap = FIRST_TAP.get((parity, group))
            if tap is not None:
                for source in range(2):
                    hit = (pick_row == 2 * tap + source) & (pick_lane == 4 * source + group)
                    pick = jnp.where(hit, 1.0, pick)
        pick = pick.astype(BF)
        for p in range(3):
            vectors[parity, p] = mm(taps[p], pick)
    pieces = []
    for row in range(FIRST):
        for parity in range(2):
            piece = jnp.zeros((channels, wide), F32)
            for p in range(3):
                piece = jnp.where(at_row == row + LEAD - 1 + p, vectors[parity, p], piece)
            pieces.append(piece.astype(BF))
    return pieces


def build_mid(taps, channels):
    wide = 8 * channels
    block = iota((channels, wide), 1) // channels
    repeat = (iota((channels, wide), 0) == iota((channels, wide), 1) % channels).astype(F32).astype(BF)
    spread_taps = mm(taps, repeat)
    pieces = []
    for row in range(2):
        for parity in range(2):
            for shifted in range(2):
                piece = jnp.zeros((channels, wide), F32)
                for p in range(3):
                    for source in range(2):
                        tap = LATER_TAP.get((shifted, parity, source))
                        if tap is not None:
                            t = 3 * p + tap
                            value = spread_taps[t * channels : (t + 1) * channels]
                            piece = jnp.where(block == 2 * (row + p) + source, value, piece)
                pieces.append(piece.astype(BF))
    return pieces


def build_last(taps, channels):
    wide = (CHUNK + 2) * 2 * channels
    lane = iota((channels, wide), 1)
    at_row = iota((CHUNK, wide), 1) // (2 * channels)
    out_row = iota((CHUNK, wide), 0)
    spread_taps = []
    for source in range(2):
        hit = (lane % channels == iota((channels, wide), 0)) & (lane // channels % 2 == source)
        spread_taps.append(mm(taps, hit.astype(F32).astype(BF)))
    pieces = []
    for shifted in range(2):
        for parity in range(2):
            piece = jnp.zeros((CHUNK, wide), F32)
            for p in range(3):
                value = jnp.zeros((1, wide), F32)
                for source in range(2):
                    tap = LATER_TAP.get((shifted, parity, source))
                    if tap is not None:
                        t = 3 * p + tap
                        value = value + spread_taps[source][t : t + 1]
                piece = jnp.where(at_row == out_row + p, value, piece)
            pieces.append(piece.astype(BF))
    return pieces


def column(row_vector, lanes):
    size = row_vector.shape[1]
    square = iota((size, size), 0) == iota((size, size), 1)
    spread_rows = jnp.where(square, jnp.broadcast_to(row_vector, (size, size)), 0.0)
    return jnp.broadcast_to(jnp.sum(spread_rows, 1, keepdims=True), (size, lanes))


def prepare_kernel(
    w0, measured, response, cos_ref, sin_ref, kin, bin_, kmid, bmid, kout,
    data_ref, first_ref, mid_ref, last_ref, bias_ref,
):
    n = response.shape[0]
    channels = kmid.shape[2]
    lanes = bias_ref.shape[3]
    cosine, sines = cos_ref[...], sin_ref[...]
    gain = 1.0 / (1.0 + response[...])
    source = (measured[0] + w0[0]).astype(BF)
    row_real = mm(source, cosine).astype(BF)
    row_imag = (-mm(source, sines)).astype(BF)
    spec_real = ((mm(cosine, row_real) + mm(sines, row_imag)) * gain).astype(BF)
    spec_imag = ((mm(cosine, row_imag) - mm(sines, row_real)) * gain).astype(BF)
    back_real = (mm(cosine, spec_real) - mm(sines, spec_imag)).astype(BF)
    back_imag = (mm(cosine, spec_imag) + mm(sines, spec_real)).astype(BF)
    data_ref[...] = (mm(back_real, cosine) - mm(back_imag, sines)) * (1.0 / (n * n))
    for which in range(3):
        for index, piece in enumerate(build_first([kin[which, p] for p in range(3)], channels)):
            first_ref[which, pl.ds(index * channels, channels), :] = piece
        for index, piece in enumerate(build_mid(kmid[which], channels)):
            mid_ref[which, pl.ds(index * channels, channels), :] = piece
        for index, piece in enumerate(build_last(kout[which], channels)):
            last_ref[which, pl.ds(index * CHUNK, CHUNK), :] = piece
        bias_ref[which, 0] = column(bin_[pl.ds(which, 1), :], lanes)
        bias_ref[which, 1] = column(bmid[pl.ds(which, 1), :], lanes)


def prepare(current, measured, response, kernel_in, bias_in, kernel_mid, bias_mid, kernel_out):
    n = response.shape[0]
    channels = bias_in.shape[1]
    lanes = n // 2
    cosine, sines = fourier_tables(n)
    kin = kernel_in.reshape(3, 3, 3, channels, 2).transpose(0, 1, 3, 2, 4).reshape(3, 3, channels, 6)
    kmid = kernel_mid[:, 0].reshape(3, 9 * channels, channels)
    bmid = bias_mid[:, 0]
    wide = (CHUNK + 2) * 2 * channels
    shapes = [
        jax.ShapeDtypeStruct((n, n), F32),
        jax.ShapeDtypeStruct((3, FIRST * 2 * channels, 8 * WINDOW), BF),
        jax.ShapeDtypeStruct((3, 8 * channels, 8 * channels), BF),
        jax.ShapeDtypeStruct((3, 4 * CHUNK, wide), BF),
        jax.ShapeDtypeStruct((3, 2, channels, lanes), F32),
    ]
    args = [response, jnp.asarray(cosine), jnp.asarray(sines), kin, bias_in, kmid, bmid, kernel_out]
    return pl.pallas_call(
        prepare_kernel,
        out_shape=shapes,
        grid=(1,),
        in_specs=[agent(0, n), agent(0, n)] + [whole(a.shape) for a in args],
        out_specs=[whole(s.shape) for s in shapes],
        cost_estimate=cost(40 * n**3, 40 * n * n),
        name="prepare",
    )(current, measured, *args)


def shifted_columns(values, parity, lanes):
    lane = iota((values.shape[0], lanes), 1)
    pieces = []
    for start in range(0, values.shape[1], lanes):
        part = values[:, start : start + lanes]
        if parity == 0:
            part = jnp.where(lane == 0, 0.0, pltpu.roll(part, 1, 1))
        else:
            part = jnp.where(lane == lanes - 1, 0.0, pltpu.roll(part, lanes - 1, 1))
        pieces.append(part)
    return jnp.concatenate(pieces, 1) if len(pieces) > 1 else pieces[0]


def halve(value):
    return jnp.maximum(value.astype(BF), jnp.zeros((), BF))


def first_layer(window, weights, bias, hidden_ref, base, channels):
    step = 8 * channels
    for index in range(FIRST * 2 * channels // step):
        product = mm(weights[pl.ds(index * step, step), :], window)
        for part in range(step // channels):
            piece = product[part * channels : (part + 1) * channels] + bias
            hidden_ref[pl.ds(base + index * step + part * channels, channels), :] = halve(piece)


def mid_layer(slab, weights, bias, out_ref, base, channels, lanes):
    product = mm(weights, slab)
    for part in range(4):
        kept = product[2 * part * channels : (2 * part + 1) * channels]
        moved = product[(2 * part + 1) * channels : (2 * part + 2) * channels]
        piece = kept + shifted_columns(moved, part % 2, lanes) + bias
        out_ref[pl.ds(base + part * channels, channels), :] = halve(piece)


def last_layer(slab, weights, lanes):
    product = mm(weights, slab)
    return [
        product[parity * CHUNK : (parity + 1) * CHUNK]
        + shifted_columns(product[(2 + parity) * CHUNK : (3 + parity) * CHUNK], parity, lanes)
        for parity in range(2)
    ]


def planes_kernel(
    frames, depth, per, channels,
    arrived_ref, first_ref, mid_ref, last_ref, bias_ref, after_ref, out_ref,
    source, result, window, hidden, deeper,
):
    lanes = arrived_ref.shape[1] // 2
    stride = 2 * per
    row = 2 * channels
    for half in range(2):
        source[half] = arrived_ref[:, half * lanes : (half + 1) * lanes].astype(F32)
    window[...] = jnp.zeros_like(window)
    for ref in (hidden, deeper):
        for k in range(2):
            ref[k, 0:row, :] = jnp.zeros((row, frames * lanes), BF)
            ref[k, pl.ds(row * (depth + 1), row), :] = jnp.zeros((row, frames * lanes), BF)

    bias1 = [jnp.concatenate([bias_ref[k + 1, 0]] * frames, 1) for k in range(2)]
    bias2 = [jnp.concatenate([bias_ref[k + 1, 1]] * frames, 1) for k in range(2)]

    def pairs(plane, _):
        for k in range(2):
            for frame in range(frames):
                base = frame * depth * stride + k * per + plane
                even = source[0, pl.ds(base, depth, stride), :]
                odd = source[1, pl.ds(base, depth, stride), :]
                groups = [even, odd, shifted_columns(even, 1, lanes), shifted_columns(odd, 0, lanes)]
                for image in range(frames):
                    channel = (frame - image) % frames
                    for group in range(4):
                        window[k, 4 * channel + group, pl.ds(LEAD, depth), pl.ds(image * lanes, lanes)] = groups[group]
        for chunk in range(depth // FIRST):
            for k in range(2):
                rows = window[k, :, pl.ds(chunk * FIRST, WINDOW), :]
                rows = rows.astype(BF).reshape(8 * WINDOW, frames * lanes)
                first_layer(rows, first_ref.at[k + 1], bias1[k], hidden.at[k], row * (1 + chunk * FIRST), channels)
        for strip in range(depth // 2):
            for k in range(2):
                slab = hidden[k, pl.ds(2 * row * strip, 4 * row), :]
                mid_layer(slab, mid_ref[k + 1], bias2[k], deeper.at[k], row * (1 + 2 * strip), channels, lanes)
        for chunk in range(depth // CHUNK):
            for k in range(2):
                slab = deeper[k, pl.ds(chunk * CHUNK * row, (CHUNK + 2) * row), :]
                parts = last_layer(slab, last_ref[k + 1], lanes)
                for half in range(2):
                    for frame in range(frames):
                        base = (frame * depth + chunk * CHUNK) * stride + k * per + plane
                        piece = parts[half][:, frame * lanes : (frame + 1) * lanes]
                        result[half, pl.ds(base, CHUNK, stride), :] = piece
        return 0

    lax.fori_loop(0, per, pairs, 0)
    for half in range(2):
        out_ref[:, half * lanes : (half + 1) * lanes] = result[half].astype(BF)


def planes(arrived, first, mid, last, bias, after, frames, depth):
    rows, n = arrived.shape
    lanes = n // 2
    channels = bias.shape[2]
    per = n // (frames * depth)
    row = 2 * channels
    args = [arrived, first, mid, last, bias]
    return pl.pallas_call(
        functools.partial(planes_kernel, frames, depth, per, channels),
        out_shape=jax.ShapeDtypeStruct((rows, n), BF),
        grid=(1,),
        in_specs=[whole(a.shape) for a in args] + [pl.BlockSpec(memory_space=pl.ANY)],
        out_specs=whole((rows, n)),
        scratch_shapes=[
            pltpu.VMEM((2, rows, lanes), F32),
            pltpu.VMEM((2, rows, lanes), F32),
            pltpu.VMEM((2, 8, depth + 2 * LEAD, frames * lanes), F32),
            pltpu.VMEM((2, row * (depth + 2), frames * lanes), BF),
            pltpu.VMEM((2, row * (depth + 2), frames * lanes), BF),
        ],
        cost_estimate=cost(2 * 9 * channels * channels * 2 * n * n * 3, 4 * n * n),
        name="planes",
    )(*args, after)


def volume_kernel(
    channels, mine_ref, other_ref, first_ref, mid_ref, last_ref, bias_ref, after_ref, out_ref,
    window, hidden, deeper,
):
    n = mine_ref.shape[0]
    lanes = n // 2
    row = 2 * channels
    depth = n // 2
    edge = row * (depth + 1)
    zeros = jnp.zeros((8, LEAD, lanes), F32)
    window[:, 0:LEAD, :] = zeros
    window[:, pl.ds(LEAD + n, LEAD), :] = zeros
    for channel, ref in enumerate((mine_ref, other_ref)):
        even = ref[:, :lanes].astype(F32)
        odd = ref[:, lanes:].astype(F32)
        groups = [even, odd, shifted_columns(even, 1, lanes), shifted_columns(odd, 0, lanes)]
        for group in range(4):
            window[4 * channel + group, pl.ds(LEAD, n), :] = groups[group]
    bias1 = jnp.concatenate([bias_ref[0, 0]] * 2, 1)
    bias2 = jnp.concatenate([bias_ref[0, 1]] * 2, 1)

    def seam(ref):
        ref[0:row, 0:lanes] = jnp.zeros((row, lanes), BF)
        ref[pl.ds(edge, row), pl.ds(lanes, lanes)] = jnp.zeros((row, lanes), BF)
        ref[0:row, pl.ds(lanes, lanes)] = ref[pl.ds(edge - row, row), 0:lanes]
        ref[pl.ds(edge, row), 0:lanes] = ref[row : 2 * row, pl.ds(lanes, lanes)]

    def first_chunk(chunk):
        halves = [
            window[:, pl.ds(pl.multiple_of(side * depth + chunk * FIRST, 8), WINDOW), :] for side in range(2)
        ]
        rows = jnp.concatenate(halves, 2).astype(BF).reshape(8 * WINDOW, 2 * lanes)
        base = pl.multiple_of(row * (1 + chunk * FIRST), row)
        first_layer(rows, first_ref.at[0], bias1, hidden, base, channels)

    def first_step(step, _):
        for inner in range(4):
            first_chunk(step * 4 + inner)
        return 0

    lax.fori_loop(0, depth // (4 * FIRST), first_step, 0)
    seam(hidden)

    def mid_step(step, _):
        for inner in range(16):
            strip = step * 16 + inner
            slab = hidden[pl.ds(pl.multiple_of(2 * row * strip, row), 4 * row), :]
            base = pl.multiple_of(row * (1 + 2 * strip), row)
            mid_layer(slab, mid_ref[0], bias2, deeper, base, channels, lanes)
        return 0

    lax.fori_loop(0, depth // 32, mid_step, 0)
    seam(deeper)

    def last_chunk(chunk):
        slab = deeper[pl.ds(pl.multiple_of(chunk * CHUNK * row, row), (CHUNK + 2) * row), :]
        parts = last_layer(slab, last_ref[0], lanes)
        for half in range(2):
            for side in range(2):
                base = pl.multiple_of(side * depth + chunk * CHUNK, CHUNK)
                piece = parts[half][:, side * lanes : (side + 1) * lanes]
                out_ref[pl.ds(base, CHUNK), pl.ds(half * lanes, lanes)] = piece.astype(BF)

    def last_step(step, _):
        for inner in range(4):
            last_chunk(step * 4 + inner)
        return 0

    lax.fori_loop(0, depth // (4 * CHUNK), last_step, 0)


def volume(mine, other, first, mid, last, bias, after):
    n = mine.shape[0]
    lanes = n // 2
    channels = bias.shape[2]
    row = 2 * channels
    args = [mine, other]
    tables = [first, mid, last, bias]
    return pl.pallas_call(
        functools.partial(volume_kernel, channels),
        out_shape=jax.ShapeDtypeStruct((n, n), BF),
        grid=(1,),
        in_specs=[whole(a.shape) for a in args]
        + [whole((1,) + t.shape[1:]) for t in tables]
        + [pl.BlockSpec(memory_space=pl.ANY)],
        out_specs=whole((n, n)),
        scratch_shapes=[
            pltpu.VMEM((8, n + 2 * LEAD, lanes), F32),
            pltpu.VMEM((row * (n // 2 + 2), n), BF),
            pltpu.VMEM((row * (n // 2 + 2), n), BF),
        ],
        cost_estimate=cost(2 * 9 * channels * channels * n * n * 3, 4 * n * n),
        name="volume",
    )(*args, *tables, after)


def combine_kernel(devices, fast, states, data, res_z, *refs):
    n = data.shape[0]
    out = refs[-1]
    split = parity_matrix(n)
    if fast:
        per = n // devices
        both = refs[0][...].astype(F32).reshape(devices, 2 * per, n)
        by_x = both[:, :per].reshape(n, n).astype(BF)
        by_y = both[:, per:].reshape(n, n).astype(BF)
    else:
        by_x, by_y = refs[0][...], refs[1][...]
    residuals = [nt(res_z[...], split), nt(split, by_x), nt(by_y, split)]
    current = [states[k] for k in range(4)]
    estimates = [data[...]] + [current[k + 1] - residuals[k] for k in range(3)]
    reflected = [2.0 * estimates[k] - current[k] for k in range(4)]
    average = (reflected[0] + reflected[1] + reflected[2] + reflected[3]) * 0.25
    for k in range(4):
        out[k] = (1.0 - relaxation) * current[k] + relaxation * (2.0 * average - reflected[k])


def combine(current, data, res_z, returned, devices):
    n = data.shape[0]
    per = n // devices
    fast = per % 8 == 0
    if fast:
        parts = [returned]
    else:
        shaped = returned.reshape(devices, 2, per, n)
        parts = [shaped[:, 0].reshape(n, n), shaped[:, 1].reshape(n, n)]
    args = [current, data, res_z] + parts
    return pl.pallas_call(
        functools.partial(combine_kernel, devices, fast),
        out_shape=jax.ShapeDtypeStruct(current.shape, F32),
        grid=(1,),
        in_specs=[whole(a.shape) for a in args],
        out_specs=whole(current.shape),
        cost_estimate=cost(6 * n**3, 40 * n * n),
        name="combine",
    )(*args)


def exchanged(rows, devices):
    n = rows.shape[1]
    blocks = rows.reshape(devices, rows.shape[0] // devices, n)
    blocks = lax.all_to_all(blocks, ("frame", "plane"), split_axis=0, concat_axis=0, tiled=True)
    return blocks.reshape(rows.shape)


def on_device(states, measured, response, kernel_in, bias_in, kernel_mid, bias_mid, kernel_out):
    frames = lax.axis_size("frame")
    depth = lax.axis_size("plane")
    devices = frames * depth
    current = states[:, 0, 0]
    mine, toward = spread(current, devices)
    other = lax.ppermute(mine, "frame", [(f, frames - 1 - f) for f in range(frames)])
    arrived = exchanged(toward, devices)
    data, first, mid, last, bias = prepare(
        current, measured[:, 0], response, kernel_in, bias_in, kernel_mid, bias_mid, kernel_out
    )
    residual = planes(arrived, first, mid, last, bias, other, frames, depth)
    returned = exchanged(residual, devices)
    res_z = volume(mine, other, first, mid, last, bias, residual)
    return combine(current, data, res_z, returned, devices)[:, None, None]


def solution(mesh):
    placed = (
        P(None, "frame", "plane", None, None),
        P("frame", "plane", None, None),
        P(),
        P(),
        P(),
        P(),
        P(),
        P(),
    )
    return jax.shard_map(
        on_device,
        mesh=mesh,
        in_specs=placed,
        out_specs=P(None, "frame", "plane", None, None),
        check_vma=False,
    )
```

```python
import functools
import math

import jax
import jax.numpy as jnp
import numpy as np
from jax import lax
from jax.experimental import pallas as pl
from jax.experimental.pallas import tpu as pltpu
from jax.sharding import PartitionSpec as P

relaxation = 0.8

BF = jnp.bfloat16
F32 = jnp.float32

CHUNK = 16
FIRST = 8
WINDOW = 16
LEAD = 4

FIRST_TAP = {(0, 3): 0, (0, 0): 1, (0, 1): 2, (1, 0): 0, (1, 1): 1, (1, 2): 2}
LATER_TAP = {
    (0, 0, 0): 1, (0, 0, 1): 2, (1, 0, 1): 0,
    (0, 1, 0): 0, (0, 1, 1): 1, (1, 1, 0): 2,
}


def fourier_tables(length):
    indices = np.arange(length, dtype=np.int64)
    phase = indices[:, None] * indices[None, :] % length
    angle = phase.astype(np.float32) * np.float32(2.0 * math.pi / length)
    return np.cos(angle).astype(BF), np.sin(angle).astype(BF)


def mm(a, b):
    return jnp.dot(a, b, preferred_element_type=F32)


def nt(a, b):
    return lax.dot_general(a, b, (((1,), (1,)), ((), ())), preferred_element_type=F32)


def tn(a, b):
    return lax.dot_general(a, b, (((0,), (0,)), ((), ())), preferred_element_type=F32)


def iota(shape, axis):
    return lax.broadcasted_iota(jnp.int32, shape, axis)


def parity_matrix(n):
    half = n // 2
    row, col = iota((n, n), 0), iota((n, n), 1)
    natural = jnp.where(col < half, 2 * col, 2 * (col - half) + 1)
    return (row == natural).astype(F32).astype(BF)


VM = pl.BlockSpec(memory_space=pltpu.VMEM)
ANYWHERE = pl.BlockSpec(memory_space=pl.ANY)
FAR = pl.BlockSpec(memory_space=pltpu.HBM)
PARAMS = pltpu.CompilerParams(vmem_limit_bytes=24 << 20)


def cost(flops, moved):
    return pl.CostEstimate(flops=flops, bytes_accessed=moved, transcendentals=0)


def spread_kernel(devices, fast, states, z_ref, *rest):
    outs, (buffer, arrival) = rest[:-2], rest[-2:]
    n = z_ref.shape[0]
    copies = [pltpu.make_async_copy(states.at[k + 1], buffer.at[k], arrival.at[k]) for k in range(3)]
    for k in (1, 2, 0):
        copies[k].start()
    split = parity_matrix(n)
    copies[1].wait()
    toward_x = tn(buffer[1].astype(BF), split)
    copies[2].wait()
    toward_y = mm(buffer[2].astype(BF), split)
    if fast:
        per = n // devices
        both = jnp.concatenate(
            [toward_x.reshape(devices, per, n), toward_y.reshape(devices, per, n)], 1
        )
        outs[0][...] = both.reshape(2 * n, n).astype(BF)
    else:
        outs[0][...] = toward_x.astype(BF)
        outs[1][...] = toward_y.astype(BF)
    copies[0].wait()
    z_ref[...] = mm(buffer[0].astype(BF), split).astype(BF)


def spread(current, devices):
    n = current.shape[1]
    per = n // devices
    fast = per % 8 == 0
    plane = jax.ShapeDtypeStruct((n, n), BF)
    shapes = [plane, jax.ShapeDtypeStruct((2 * n, n), BF)] if fast else [plane] * 3
    outs = pl.pallas_call(
        functools.partial(spread_kernel, devices, fast),
        out_shape=shapes,
        in_specs=[FAR],
        out_specs=[VM] * len(shapes),
        scratch_shapes=[pltpu.VMEM((3, n, n), F32), pltpu.SemaphoreType.DMA((3,))],
        compiler_params=PARAMS,
        cost_estimate=cost(6 * n**3, 18 * n * n),
        name="spread",
    )(current)
    if fast:
        return outs[0], outs[1]
    parts = [o.reshape(devices, per, n) for o in outs[1:]]
    return outs[0], jnp.concatenate(parts, 1).reshape(2 * n, n)


def build_first(taps, channels):
    wide = 8 * WINDOW
    lane = iota((channels, wide), 1)
    at_row = lane % WINDOW
    pick_row = iota((6, wide), 0)
    pick_lane = iota((6, wide), 1) // WINDOW
    vectors = {}
    for parity in range(2):
        pick = jnp.zeros((6, wide), F32)
        for group in range(4):
            tap = FIRST_TAP.get((parity, group))
            if tap is not None:
                for source in range(2):
                    hit = (pick_row == 2 * tap + source) & (pick_lane == 4 * source + group)
                    pick = jnp.where(hit, 1.0, pick)
        pick = pick.astype(BF)
        for p in range(3):
            vectors[parity, p] = mm(taps[p], pick)
    pieces = []
    for row in range(FIRST):
        for parity in range(2):
            piece = jnp.zeros((channels, wide), F32)
            for p in range(3):
                piece = jnp.where(at_row == row + LEAD - 1 + p, vectors[parity, p], piece)
            pieces.append(piece.astype(BF))
    return pieces


def build_mid(taps, channels):
    wide = 8 * channels
    block = iota((channels, wide), 1) // channels
    repeat = (iota((channels, wide), 0) == iota((channels, wide), 1) % channels).astype(F32).astype(BF)
    spread_taps = mm(taps, repeat)
    pieces = []
    for row in range(2):
        for parity in range(2):
            for shifted in range(2):
                piece = jnp.zeros((channels, wide), F32)
                for p in range(3):
                    for source in range(2):
                        tap = LATER_TAP.get((shifted, parity, source))
                        if tap is not None:
                            t = 3 * p + tap
                            value = spread_taps[t * channels : (t + 1) * channels]
                            piece = jnp.where(block == 2 * (row + p) + source, value, piece)
                pieces.append(piece.astype(BF))
    return pieces


def build_last(taps, channels):
    wide = (CHUNK + 2) * 2 * channels
    lane = iota((channels, wide), 1)
    at_row = iota((CHUNK, wide), 1) // (2 * channels)
    out_row = iota((CHUNK, wide), 0)
    spread_taps = []
    for source in range(2):
        hit = (lane % channels == iota((channels, wide), 0)) & (lane // channels % 2 == source)
        spread_taps.append(mm(taps, hit.astype(F32).astype(BF)))
    pieces = []
    for shifted in range(2):
        for parity in range(2):
            piece = jnp.zeros((CHUNK, wide), F32)
            for p in range(3):
                value = jnp.zeros((1, wide), F32)
                for source in range(2):
                    tap = LATER_TAP.get((shifted, parity, source))
                    if tap is not None:
                        t = 3 * p + tap
                        value = value + spread_taps[source][t : t + 1]
                piece = jnp.where(at_row == out_row + p, value, piece)
            pieces.append(piece.astype(BF))
    return pieces


def column(row_vector, lanes):
    size = row_vector.shape[1]
    square = iota((size, size), 0) == iota((size, size), 1)
    spread_rows = jnp.where(square, jnp.broadcast_to(row_vector, (size, size)), 0.0)
    return jnp.broadcast_to(jnp.sum(spread_rows, 1, keepdims=True), (size, lanes))


def prepare_kernel(
    states, measured, response, cos_ref, sin_ref, kin, bin_, kmid, bmid, kout,
    data_ref, first_ref, mid_ref, last_ref, bias_ref, w0, arrival,
):
    copy = pltpu.make_async_copy(states.at[0], w0, arrival)
    copy.start()
    n = response.shape[0]
    channels = kmid.shape[2]
    lanes = bias_ref.shape[3]
    cosine, sines = cos_ref[...], sin_ref[...]
    gain = 1.0 / (1.0 + response[...])
    copy.wait()
    source = (measured[0] + w0[...]).astype(BF)
    row_real = mm(source, cosine).astype(BF)
    row_imag = (-mm(source, sines)).astype(BF)
    spec_real = ((mm(cosine, row_real) + mm(sines, row_imag)) * gain).astype(BF)
    spec_imag = ((mm(cosine, row_imag) - mm(sines, row_real)) * gain).astype(BF)
    back_real = (mm(cosine, spec_real) - mm(sines, spec_imag)).astype(BF)
    back_imag = (mm(cosine, spec_imag) + mm(sines, spec_real)).astype(BF)
    data_ref[...] = (mm(back_real, cosine) - mm(back_imag, sines)) * (1.0 / (n * n))
    for which in range(3):
        for index, piece in enumerate(build_first([kin[which, p] for p in range(3)], channels)):
            first_ref[which, pl.ds(index * channels, channels), :] = piece
        for index, piece in enumerate(build_mid(kmid[which], channels)):
            mid_ref[which, pl.ds(index * channels, channels), :] = piece
        for index, piece in enumerate(build_last(kout[which], channels)):
            last_ref[which, pl.ds(index * CHUNK, CHUNK), :] = piece
        bias_ref[which, 0] = column(bin_[pl.ds(which, 1), :], lanes)
        bias_ref[which, 1] = column(bmid[pl.ds(which, 1), :], lanes)


def prepare(current, measured, response, kernel_in, bias_in, kernel_mid, bias_mid, kernel_out):
    n = response.shape[0]
    channels = bias_in.shape[1]
    lanes = n // 2
    cosine, sines = fourier_tables(n)
    kin = kernel_in.reshape(3, 3, 3, channels, 2).transpose(0, 1, 3, 2, 4).reshape(3, 3, channels, 6)
    kmid = kernel_mid[:, 0].reshape(3, 9 * channels, channels)
    bmid = bias_mid[:, 0]
    wide = (CHUNK + 2) * 2 * channels
    shapes = [
        jax.ShapeDtypeStruct((n, n), F32),
        jax.ShapeDtypeStruct((3, FIRST * 2 * channels, 8 * WINDOW), BF),
        jax.ShapeDtypeStruct((3, 8 * channels, 8 * channels), BF),
        jax.ShapeDtypeStruct((3, 4 * CHUNK, wide), BF),
        jax.ShapeDtypeStruct((3, 2, channels, lanes), F32),
    ]
    args = [response, jnp.asarray(cosine), jnp.asarray(sines), kin, bias_in, kmid, bmid, kernel_out]
    return pl.pallas_call(
        prepare_kernel,
        out_shape=shapes,
        in_specs=[FAR] + [VM] * (len(args) + 1),
        out_specs=[VM] * len(shapes),
        scratch_shapes=[pltpu.VMEM((n, n), F32), pltpu.SemaphoreType.DMA],
        compiler_params=PARAMS,
        cost_estimate=cost(40 * n**3, 40 * n * n),
        name="prepare",
    )(current, measured, *args)


def shifted_columns(values, parity, lanes):
    lane = iota((values.shape[0], lanes), 1)
    zero = jnp.zeros((), values.dtype)
    pieces = []
    for start in range(0, values.shape[1], lanes):
        part = values[:, start : start + lanes]
        if parity == 0:
            part = jnp.where(lane == 0, zero, pltpu.roll(part, 1, 1))
        else:
            part = jnp.where(lane == lanes - 1, zero, pltpu.roll(part, lanes - 1, 1))
        pieces.append(part)
    return jnp.concatenate(pieces, 1) if len(pieces) > 1 else pieces[0]


def halve(value):
    return jnp.maximum(value.astype(BF), jnp.zeros((), BF))


def first_layer(window, weights, bias, hidden_ref, base, channels):
    step = 8 * channels
    for index in range(FIRST * 2 * channels // step):
        product = mm(weights[pl.ds(index * step, step), :], window)
        for part in range(step // channels):
            piece = product[part * channels : (part + 1) * channels] + bias
            hidden_ref[pl.ds(base + index * step + part * channels, channels), :] = halve(piece)


def mid_layer(slab, weights, bias, out_ref, base, channels, lanes):
    product = mm(weights, slab)
    for part in range(4):
        kept = product[2 * part * channels : (2 * part + 1) * channels]
        moved = product[(2 * part + 1) * channels : (2 * part + 2) * channels]
        piece = (kept + bias).astype(BF) + shifted_columns(moved.astype(BF), part % 2, lanes)
        out_ref[pl.ds(base + part * channels, channels), :] = jnp.maximum(piece, jnp.zeros((), BF))


def last_layer(slab, weights, lanes):
    product = mm(weights, slab)
    return [
        product[parity * CHUNK : (parity + 1) * CHUNK]
        + shifted_columns(product[(2 + parity) * CHUNK : (3 + parity) * CHUNK], parity, lanes)
        for parity in range(2)
    ]


def planes_kernel(
    frames, depth, per, channels,
    arrived_ref, first_ref, mid_ref, last_ref, bias_ref, out_ref,
    source, result, window, hidden, deeper,
):
    lanes = arrived_ref.shape[1] // 2
    stride = 2 * per
    row = 2 * channels
    for half in range(2):
        source[half] = arrived_ref[:, half * lanes : (half + 1) * lanes].astype(F32)
    for slot in range(window.shape[0]):
        window[slot, :, 0:LEAD, :] = jnp.zeros((8, LEAD, frames * lanes), F32)
        window[slot, :, pl.ds(LEAD + depth, LEAD), :] = jnp.zeros((8, LEAD, frames * lanes), F32)
    for ref in (hidden, deeper):
        for slot in range(ref.shape[0]):
            ref[slot, 0:row, :] = jnp.zeros((row, frames * lanes), BF)
            ref[slot, pl.ds(row * (depth + 1), row), :] = jnp.zeros((row, frames * lanes), BF)
    bias1 = [jnp.concatenate([bias_ref[k + 1, 0]] * frames, 1) for k in range(2)]
    bias2 = [jnp.concatenate([bias_ref[k + 1, 1]] * frames, 1) for k in range(2)]

    def fill(items):
        for slot, k, plane in items:
            for frame in range(frames):
                base = frame * depth * stride + k * per + plane
                even = source[0, pl.ds(base, depth, stride), :]
                odd = source[1, pl.ds(base, depth, stride), :]
                groups = [even, odd, shifted_columns(even, 1, lanes), shifted_columns(odd, 0, lanes)]
                for image in range(frames):
                    channel = (frame - image) % frames
                    for group in range(4):
                        window[slot, 4 * channel + group, pl.ds(LEAD, depth), pl.ds(image * lanes, lanes)] = groups[group]

    def enter(items):
        for chunk in range(depth // FIRST):
            for slot, k, plane in items:
                rows = window[slot, :, pl.ds(chunk * FIRST, WINDOW), :]
                rows = rows.astype(BF).reshape(8 * WINDOW, frames * lanes)
                first_layer(rows, first_ref.at[k + 1], bias1[k], hidden.at[slot], row * (1 + chunk * FIRST), channels)

    def cross(items):
        for strip in range(depth // 2):
            for slot, k, plane in items:
                slab = hidden[slot, pl.ds(2 * row * strip, 4 * row), :]
                mid_layer(slab, mid_ref[k + 1], bias2[k], deeper.at[slot], row * (1 + 2 * strip), channels, lanes)

    def leave(items):
        for chunk in range(depth // CHUNK):
            for slot, k, plane in items:
                slab = deeper[slot, pl.ds(chunk * CHUNK * row, (CHUNK + 2) * row), :]
                parts = last_layer(slab, last_ref[k + 1], lanes)
                for half in range(2):
                    for frame in range(frames):
                        base = (frame * depth + chunk * CHUNK) * stride + k * per + plane
                        piece = parts[half][:, frame * lanes : (frame + 1) * lanes]
                        result[half, pl.ds(base, CHUNK, stride), :] = piece

    batches = [
        [(2 * (plane % 2) + k, k, plane) for k in range(2)] for plane in range(per)
    ]
    fill(batches[0])
    enter(batches[0])
    for index, items in enumerate(batches):
        coming = batches[index + 1 : index + 2]
        for batch in coming:
            fill(batch)
        cross(items)
        for batch in coming:
            enter(batch)
        leave(items)
    for half in range(2):
        out_ref[:, half * lanes : (half + 1) * lanes] = result[half].astype(BF)


def planes(arrived, first, mid, last, bias, frames, depth):
    rows, n = arrived.shape
    lanes = n // 2
    channels = bias.shape[2]
    per = n // (frames * depth)
    row = 2 * channels
    args = [arrived, first, mid, last, bias]
    return pl.pallas_call(
        functools.partial(planes_kernel, frames, depth, per, channels),
        out_shape=jax.ShapeDtypeStruct((rows, n), BF),
        in_specs=[VM] * len(args),
        out_specs=VM,
        compiler_params=PARAMS,
        scratch_shapes=[
            pltpu.VMEM((2, rows, lanes), F32),
            pltpu.VMEM((2, rows, lanes), F32),
            pltpu.VMEM((4, 8, depth + 2 * LEAD, frames * lanes), F32),
            pltpu.VMEM((4, row * (depth + 2), frames * lanes), BF),
            pltpu.VMEM((4, row * (depth + 2), frames * lanes), BF),
        ],
        cost_estimate=cost(2 * 9 * channels * channels * 2 * n * n * 3, 4 * n * n),
        name="planes",
    )(*args)


def volume_kernel(
    channels, mine_ref, other_ref, first_ref, mid_ref, last_ref, bias_ref, states, data, after_ref, out_ref,
    window, hidden, deeper, residual, held, arrival,
):
    copy = pltpu.make_async_copy(states, held, arrival)
    copy.start()
    n = mine_ref.shape[0]
    lanes = n // 2
    row = 2 * channels
    depth = n // 2
    edge = row * (depth + 1)
    zeros = jnp.zeros((8, LEAD, lanes), F32)
    window[:, 0:LEAD, :] = zeros
    window[:, pl.ds(LEAD + n, LEAD), :] = zeros
    for channel, ref in enumerate((mine_ref, other_ref)):
        even = ref[:, :lanes].astype(F32)
        odd = ref[:, lanes:].astype(F32)
        groups = [even, odd, shifted_columns(even, 1, lanes), shifted_columns(odd, 0, lanes)]
        for group in range(4):
            window[4 * channel + group, pl.ds(LEAD, n), :] = groups[group]
    bias1 = jnp.concatenate([bias_ref[0, 0]] * 2, 1)
    bias2 = jnp.concatenate([bias_ref[0, 1]] * 2, 1)

    def seam(ref):
        ref[0:row, 0:lanes] = jnp.zeros((row, lanes), BF)
        ref[pl.ds(edge, row), pl.ds(lanes, lanes)] = jnp.zeros((row, lanes), BF)
        ref[0:row, pl.ds(lanes, lanes)] = ref[pl.ds(edge - row, row), 0:lanes]
        ref[pl.ds(edge, row), 0:lanes] = ref[row : 2 * row, pl.ds(lanes, lanes)]

    def first_chunk(chunk):
        halves = [
            window[:, pl.ds(pl.multiple_of(side * depth + chunk * FIRST, 8), WINDOW), :] for side in range(2)
        ]
        rows = jnp.concatenate(halves, 2).astype(BF).reshape(8 * WINDOW, 2 * lanes)
        base = pl.multiple_of(row * (1 + chunk * FIRST), row)
        first_layer(rows, first_ref.at[0], bias1, hidden, base, channels)

    def first_step(step, _):
        for inner in range(4):
            first_chunk(step * 4 + inner)
        return 0

    lax.fori_loop(0, depth // (4 * FIRST), first_step, 0)
    seam(hidden)

    def mid_step(step, _):
        for inner in range(16):
            strip = step * 16 + inner
            slab = hidden[pl.ds(pl.multiple_of(2 * row * strip, row), 4 * row), :]
            base = pl.multiple_of(row * (1 + 2 * strip), row)
            mid_layer(slab, mid_ref[0], bias2, deeper, base, channels, lanes)
        return 0

    lax.fori_loop(0, depth // 32, mid_step, 0)
    seam(deeper)

    def last_chunk(chunk):
        slab = deeper[pl.ds(pl.multiple_of(chunk * CHUNK * row, row), (CHUNK + 2) * row), :]
        parts = last_layer(slab, last_ref[0], lanes)
        for half in range(2):
            for side in range(2):
                base = pl.multiple_of(side * depth + chunk * CHUNK, CHUNK)
                piece = parts[half][:, side * lanes : (side + 1) * lanes]
                residual[pl.ds(base, CHUNK), pl.ds(half * lanes, lanes)] = piece.astype(BF)

    def last_step(step, _):
        for inner in range(4):
            last_chunk(step * 4 + inner)
        return 0

    lax.fori_loop(0, depth // (4 * CHUNK), last_step, 0)

    copy.wait()
    current = [held[k] for k in range(4)]
    estimates = [data[...], current[1] - nt(residual[...], parity_matrix(n)), current[2], current[3]]
    reflected = [2.0 * estimates[k] - current[k] for k in range(4)]
    average = (reflected[0] + reflected[1] + reflected[2] + reflected[3]) * 0.25
    for k in range(4):
        out_ref[k] = (1.0 - relaxation) * current[k] + relaxation * (2.0 * average - reflected[k])


def volume(mine, other, first, mid, last, bias, current, data, after):
    n = mine.shape[0]
    lanes = n // 2
    channels = bias.shape[2]
    row = 2 * channels
    args = [mine, other, first, mid, last, bias, current, data, after]
    return pl.pallas_call(
        functools.partial(volume_kernel, channels),
        out_shape=jax.ShapeDtypeStruct(current.shape, F32),
        in_specs=[VM] * 6 + [FAR, VM, ANYWHERE],
        out_specs=VM,
        compiler_params=PARAMS,
        scratch_shapes=[
            pltpu.VMEM((8, n + 2 * LEAD, lanes), F32),
            pltpu.VMEM((row * (n // 2 + 2), n), BF),
            pltpu.VMEM((row * (n // 2 + 2), n), BF),
            pltpu.VMEM((n, n), BF),
            pltpu.VMEM(current.shape, F32),
            pltpu.SemaphoreType.DMA,
        ],
        cost_estimate=cost(2 * 9 * channels * channels * n * n * 3, 4 * n * n),
        name="volume",
    )(*args)


def combine_kernel(devices, fast, partial, *refs):
    out, buffer, departure = refs[-3:]
    n = partial.shape[1]
    split = parity_matrix(n)
    if fast:
        per = n // devices
        both = refs[0][...].astype(F32).reshape(devices, 2 * per, n)
        by_x = both[:, :per].reshape(n, n).astype(BF)
        by_y = both[:, per:].reshape(n, n).astype(BF)
    else:
        by_x, by_y = refs[0][...], refs[1][...]
    blocks = 2
    size = n // blocks
    copies = []
    for block in range(blocks):
        rows = slice(block * size, (block + 1) * size)
        res_x = nt(split[rows], by_x)
        res_y = nt(by_y[rows], split)
        common = -relaxation * (res_x + res_y)
        steps = [common, common, common + 2.0 * relaxation * res_x, common + 2.0 * relaxation * res_y]
        for k in range(4):
            buffer[k, rows] = partial[k, rows] + steps[k]
            copy = pltpu.make_async_copy(buffer.at[k, rows], out.at[k, rows], departure.at[block, k])
            copy.start()
            copies.append(copy)
    for copy in copies:
        copy.wait()


def combine(partial, returned, devices):
    n = partial.shape[1]
    per = n // devices
    fast = per % 8 == 0
    if fast:
        parts = [returned]
    else:
        shaped = returned.reshape(devices, 2, per, n)
        parts = [shaped[:, 0].reshape(n, n), shaped[:, 1].reshape(n, n)]
    args = [partial] + parts
    return pl.pallas_call(
        functools.partial(combine_kernel, devices, fast),
        out_shape=jax.ShapeDtypeStruct(partial.shape, F32),
        in_specs=[VM] * len(args),
        out_specs=FAR,
        scratch_shapes=[pltpu.VMEM(partial.shape, F32), pltpu.SemaphoreType.DMA((2, 4))],
        compiler_params=PARAMS,
        cost_estimate=cost(6 * n**3, 40 * n * n),
        name="combine",
    )(*args)


def exchanged(rows, devices):
    n = rows.shape[1]
    blocks = rows.reshape(devices, rows.shape[0] // devices, n)
    blocks = lax.all_to_all(blocks, ("frame", "plane"), split_axis=0, concat_axis=0, tiled=True)
    return blocks.reshape(rows.shape)


def on_device(states, measured, response, kernel_in, bias_in, kernel_mid, bias_mid, kernel_out):
    frames = lax.axis_size("frame")
    depth = lax.axis_size("plane")
    devices = frames * depth
    current = pltpu.with_memory_space_constraint(states[:, 0, 0], pltpu.HBM)
    mine, toward = spread(current, devices)
    other = lax.ppermute(mine, "frame", [(f, frames - 1 - f) for f in range(frames)])
    arrived = exchanged(toward, devices)
    data, first, mid, last, bias = prepare(
        current, measured[:, 0], response, kernel_in, bias_in, kernel_mid, bias_mid, kernel_out
    )
    arrived, other = lax.optimization_barrier((arrived, other))
    residual = planes(arrived, first, mid, last, bias, frames, depth)
    returned = exchanged(residual, devices)
    partial = volume(mine, other, first, mid, last, bias, current, data, residual)
    return combine(partial, returned, devices)[:, None, None]


def solution(mesh):
    placed = (
        P(None, "frame", "plane", None, None),
        P("frame", "plane", None, None),
        P(),
        P(),
        P(),
        P(),
        P(),
        P(),
    )
    return jax.shard_map(
        on_device,
        mesh=mesh,
        in_specs=placed,
        out_specs=P(None, "frame", "plane", None, None),
        check_vma=False,
    )
```

```python
import functools
import math

import jax
import jax.numpy as jnp
import numpy as np
from jax import lax
from jax.experimental import pallas as pl
from jax.experimental.pallas import tpu as pltpu
from jax.sharding import PartitionSpec as P

relaxation = 0.8

BF = jnp.bfloat16
F32 = jnp.float32

CHUNK = 16
FIRST = 8
WINDOW = 16
LEAD = 4
PIECE = 4
SPLIT = 1

FIRST_TAP = {(0, 3): 0, (0, 0): 1, (0, 1): 2, (1, 0): 0, (1, 1): 1, (1, 2): 2}
LATER_TAP = {
    (0, 0, 0): 1, (0, 0, 1): 2, (1, 0, 1): 0,
    (0, 1, 0): 0, (0, 1, 1): 1, (1, 1, 0): 2,
}


def fourier_tables(length):
    indices = np.arange(length, dtype=np.int64)
    phase = indices[:, None] * indices[None, :] % length
    angle = phase.astype(np.float32) * np.float32(2.0 * math.pi / length)
    return np.cos(angle).astype(BF), np.sin(angle).astype(BF)


def mm(a, b):
    return jnp.dot(a, b, preferred_element_type=F32)


def nt(a, b):
    return lax.dot_general(a, b, (((1,), (1,)), ((), ())), preferred_element_type=F32)


def tn(a, b):
    return lax.dot_general(a, b, (((0,), (0,)), ((), ())), preferred_element_type=F32)


def iota(shape, axis):
    return lax.broadcasted_iota(jnp.int32, shape, axis)


def parity_matrix(n):
    half = n // 2
    row, col = iota((n, n), 0), iota((n, n), 1)
    natural = jnp.where(col < half, 2 * col, 2 * (col - half) + 1)
    return (row == natural).astype(F32).astype(BF)


VM = pl.BlockSpec(memory_space=pltpu.VMEM)
ANYWHERE = pl.BlockSpec(memory_space=pl.ANY)
FAR = pl.BlockSpec(memory_space=pltpu.HBM)
PARAMS = pltpu.CompilerParams(vmem_limit_bytes=24 << 20)
PLANES = pltpu.CompilerParams(
    vmem_limit_bytes=24 << 20
)


def cost(flops, moved):
    return pl.CostEstimate(flops=flops, bytes_accessed=moved, transcendentals=0)


def spread_kernel(devices, fast, states, *rest):
    outs, (buffer, arrival) = rest[:-2], rest[-2:]
    n = states.shape[1]
    copies = [pltpu.make_async_copy(states.at[k + 2], buffer.at[k], arrival.at[k]) for k in range(2)]
    for copy in copies:
        copy.start()
    split = parity_matrix(n)
    copies[0].wait()
    toward_x = tn(buffer[0].astype(BF), split)
    copies[1].wait()
    toward_y = mm(buffer[1].astype(BF), split)
    if fast:
        per = n // devices
        both = jnp.concatenate(
            [toward_x.reshape(devices, per, n), toward_y.reshape(devices, per, n)], 1
        )
        outs[0][...] = both.reshape(2 * n, n).astype(BF)
    else:
        outs[0][...] = toward_x.astype(BF)
        outs[1][...] = toward_y.astype(BF)


def spread(current, devices):
    n = current.shape[1]
    per = n // devices
    fast = per % 8 == 0
    shapes = [jax.ShapeDtypeStruct((2 * n, n), BF)] if fast else [jax.ShapeDtypeStruct((n, n), BF)] * 2
    outs = pl.pallas_call(
        functools.partial(spread_kernel, devices, fast),
        out_shape=shapes,
        in_specs=[FAR],
        out_specs=[VM] * len(shapes),
        scratch_shapes=[pltpu.VMEM((2, n, n), F32), pltpu.SemaphoreType.DMA((2,))],
        compiler_params=PARAMS,
        cost_estimate=cost(4 * n**3, 12 * n * n),
        name="spread",
    )(current)
    if fast:
        return outs[0]
    parts = [o.reshape(devices, per, n) for o in outs]
    return jnp.concatenate(parts, 1).reshape(2 * n, n)


def mine_kernel(states, out_ref, buffer, arrival):
    copy = pltpu.make_async_copy(states.at[1], buffer, arrival)
    copy.start()
    split = parity_matrix(out_ref.shape[0])
    copy.wait()
    out_ref[...] = mm(buffer[...].astype(BF), split).astype(BF)


def own_plane(current):
    n = current.shape[1]
    return pl.pallas_call(
        mine_kernel,
        out_shape=jax.ShapeDtypeStruct((n, n), BF),
        in_specs=[FAR],
        out_specs=VM,
        scratch_shapes=[pltpu.VMEM((n, n), F32), pltpu.SemaphoreType.DMA],
        compiler_params=PARAMS,
        cost_estimate=cost(2 * n**3, 6 * n * n),
        name="own_plane",
    )(current)


def build_first(taps, channels):
    wide = 8 * WINDOW
    lane = iota((channels, wide), 1)
    at_row = lane % WINDOW
    pick_row = iota((6, wide), 0)
    pick_lane = iota((6, wide), 1) // WINDOW
    vectors = {}
    for parity in range(2):
        pick = jnp.zeros((6, wide), F32)
        for group in range(4):
            tap = FIRST_TAP.get((parity, group))
            if tap is not None:
                for source in range(2):
                    hit = (pick_row == 2 * tap + source) & (pick_lane == 4 * source + group)
                    pick = jnp.where(hit, 1.0, pick)
        pick = pick.astype(BF)
        for p in range(3):
            vectors[parity, p] = mm(taps[p], pick)
    pieces = []
    for row in range(FIRST):
        for parity in range(2):
            piece = jnp.zeros((channels, wide), F32)
            for p in range(3):
                piece = jnp.where(at_row == row + LEAD - 1 + p, vectors[parity, p], piece)
            pieces.append(piece.astype(BF))
    return pieces


def build_mid(taps, channels):
    wide = 8 * channels
    block = iota((channels, wide), 1) // channels
    repeat = (iota((channels, wide), 0) == iota((channels, wide), 1) % channels).astype(F32).astype(BF)
    spread_taps = mm(taps, repeat)
    pieces = []
    for row in range(2):
        for parity in range(2):
            for shifted in range(2):
                piece = jnp.zeros((channels, wide), F32)
                for p in range(3):
                    for source in range(2):
                        tap = LATER_TAP.get((shifted, parity, source))
                        if tap is not None:
                            t = 3 * p + tap
                            value = spread_taps[t * channels : (t + 1) * channels]
                            piece = jnp.where(block == 2 * (row + p) + source, value, piece)
                pieces.append(piece.astype(BF))
    return pieces


def build_last(taps, channels):
    wide = (CHUNK + 2) * 2 * channels
    lane = iota((channels, wide), 1)
    at_row = iota((CHUNK, wide), 1) // (2 * channels)
    out_row = iota((CHUNK, wide), 0)
    spread_taps = []
    for source in range(2):
        hit = (lane % channels == iota((channels, wide), 0)) & (lane // channels % 2 == source)
        spread_taps.append(mm(taps, hit.astype(F32).astype(BF)))
    pieces = []
    for shifted in range(2):
        for parity in range(2):
            piece = jnp.zeros((CHUNK, wide), F32)
            for p in range(3):
                value = jnp.zeros((1, wide), F32)
                for source in range(2):
                    tap = LATER_TAP.get((shifted, parity, source))
                    if tap is not None:
                        t = 3 * p + tap
                        value = value + spread_taps[source][t : t + 1]
                piece = jnp.where(at_row == out_row + p, value, piece)
            pieces.append(piece)
    return pieces


def column(row_vector, lanes):
    size = row_vector.shape[1]
    square = iota((size, size), 0) == iota((size, size), 1)
    spread_rows = jnp.where(square, jnp.broadcast_to(row_vector, (size, size)), 0.0)
    return jnp.broadcast_to(jnp.sum(spread_rows, 1, keepdims=True), (size, lanes))


def prepare_kernel(
    states, measured, response, cos_ref, sin_ref, kin, bin_, kmid, bmid, kout,
    data_ref, first_ref, mid_ref, last_ref, inner_ref, bias_ref, w0, arrival,
):
    copy = pltpu.make_async_copy(states.at[0], w0, arrival)
    copy.start()
    n = response.shape[0]
    channels = kmid.shape[2]
    lanes = bias_ref.shape[3]
    cosine, sines = cos_ref[...], sin_ref[...]
    gain = 1.0 / (1.0 + response[...])
    copy.wait()
    source = (measured[0] + w0[...]).astype(BF)
    row_real = mm(source, cosine).astype(BF)
    row_imag = (-mm(source, sines)).astype(BF)
    spec_real = ((mm(cosine, row_real) + mm(sines, row_imag)) * gain).astype(BF)
    spec_imag = ((mm(cosine, row_imag) - mm(sines, row_real)) * gain).astype(BF)
    back_real = (mm(cosine, spec_real) - mm(sines, spec_imag)).astype(BF)
    back_imag = (mm(cosine, spec_imag) + mm(sines, spec_real)).astype(BF)
    data_ref[...] = (mm(back_real, cosine) - mm(back_imag, sines)) * (1.0 / (n * n))
    for which in range(3):
        for index, piece in enumerate(build_first([kin[which, p] for p in range(3)], channels)):
            first_ref[which, pl.ds(index * channels, channels), :] = piece
        for index, piece in enumerate(build_mid(kmid[which], channels)):
            mid_ref[which, pl.ds(index * channels, channels), :] = piece
        for index, piece in enumerate(build_last(kout[which], channels)):
            last_ref[which, pl.ds(index * CHUNK, CHUNK), :] = piece.astype(BF)
            inner = piece[:, 2 * channels : 2 * channels * (CHUNK + 1)]
            inner_ref[which, pl.ds(index * CHUNK, CHUNK), :] = inner.astype(BF)
        bias_ref[which, 0] = column(bin_[pl.ds(which, 1), :], lanes)
        bias_ref[which, 1] = column(bmid[pl.ds(which, 1), :], lanes)


def prepare(current, measured, response, kernel_in, bias_in, kernel_mid, bias_mid, kernel_out):
    n = response.shape[0]
    channels = bias_in.shape[1]
    lanes = n // 2
    cosine, sines = fourier_tables(n)
    kin = kernel_in.reshape(3, 3, 3, channels, 2).transpose(0, 1, 3, 2, 4).reshape(3, 3, channels, 6)
    kmid = kernel_mid[:, 0].reshape(3, 9 * channels, channels)
    bmid = bias_mid[:, 0]
    wide = (CHUNK + 2) * 2 * channels
    shapes = [
        jax.ShapeDtypeStruct((n, n), F32),
        jax.ShapeDtypeStruct((3, FIRST * 2 * channels, 8 * WINDOW), BF),
        jax.ShapeDtypeStruct((3, 8 * channels, 8 * channels), BF),
        jax.ShapeDtypeStruct((3, 4 * CHUNK, wide), BF),
        jax.ShapeDtypeStruct((3, 4 * CHUNK, CHUNK * 2 * channels), BF),
        jax.ShapeDtypeStruct((3, 2, channels, lanes), F32),
    ]
    args = [response, jnp.asarray(cosine), jnp.asarray(sines), kin, bias_in, kmid, bmid, kernel_out]
    return pl.pallas_call(
        prepare_kernel,
        out_shape=shapes,
        in_specs=[FAR] + [VM] * (len(args) + 1),
        out_specs=[VM] * len(shapes),
        scratch_shapes=[pltpu.VMEM((n, n), F32), pltpu.SemaphoreType.DMA],
        compiler_params=PARAMS,
        cost_estimate=cost(40 * n**3, 40 * n * n),
        name="prepare",
    )(current, measured, *args)


def shifted_columns(values, parity, lanes):
    lane = iota((values.shape[0], lanes), 1)
    zero = jnp.zeros((), values.dtype)
    pieces = []
    for start in range(0, values.shape[1], lanes):
        part = values[:, start : start + lanes]
        if parity == 0:
            part = jnp.where(lane == 0, zero, pltpu.roll(part, 1, 1))
        else:
            part = jnp.where(lane == lanes - 1, zero, pltpu.roll(part, lanes - 1, 1))
        pieces.append(part)
    return jnp.concatenate(pieces, 1) if len(pieces) > 1 else pieces[0]


def halve(value):
    return jnp.maximum(value.astype(BF), jnp.zeros((), BF))


def first_layer(window, weights, bias, hidden_ref, base, channels):
    step = PIECE * channels

    def piece(index):
        product = mm(weights[pl.ds(index * step, step), :], window())
        for part in range(step // channels):
            rows = product[part * channels : (part + 1) * channels] + bias
            hidden_ref[pl.ds(base + index * step + part * channels, channels), :] = halve(rows)

    return [functools.partial(piece, index) for index in range(FIRST * 2 * channels // step)]


def mid_layer(slab, weights, bias, out_ref, base, channels, lanes):
    parts = 4 // SPLIT
    step = 2 * parts * channels
    for index in range(SPLIT):
        product = mm(weights[pl.ds(index * step, step), :], slab())
        for part in range(parts):
            kept = product[2 * part * channels : (2 * part + 1) * channels]
            moved = product[(2 * part + 1) * channels : (2 * part + 2) * channels]
            piece = kept + shifted_columns(moved, part % 2 if parts > 1 else index % 2, lanes) + bias
            out_ref[pl.ds(base + (index * parts + part) * channels, channels), :] = halve(piece)


def last_layer(slab, weights, lanes):
    product = mm(weights, slab)
    return [
        product[parity * CHUNK : (parity + 1) * CHUNK]
        + shifted_columns(product[(2 + parity) * CHUNK : (3 + parity) * CHUNK], parity, lanes)
        for parity in range(2)
    ]


def planes_kernel(
    frames, depth, per, channels,
    arrived_ref, first_ref, mid_ref, last_ref, bias_ref, out_ref,
    source, result, window, hidden, deeper,
):
    lanes = arrived_ref.shape[1] // 2
    stride = 2 * per
    row = 2 * channels
    for half in range(2):
        source[half] = arrived_ref[:, half * lanes : (half + 1) * lanes].astype(F32)
    for slot in range(window.shape[0]):
        window[slot, :, 0:LEAD, :] = jnp.zeros((8, LEAD, frames * lanes), F32)
        window[slot, :, pl.ds(LEAD + depth, LEAD), :] = jnp.zeros((8, LEAD, frames * lanes), F32)
    for ref in (hidden, deeper):
        for slot in range(ref.shape[0]):
            ref[slot, 0:row, :] = jnp.zeros((row, frames * lanes), BF)
            ref[slot, pl.ds(row * (depth + 1), row), :] = jnp.zeros((row, frames * lanes), BF)
    bias1 = [jnp.concatenate([bias_ref[k + 1, 0]] * frames, 1) for k in range(2)]
    bias2 = [jnp.concatenate([bias_ref[k + 1, 1]] * frames, 1) for k in range(2)]

    def fill(items):
        for slot, k, plane in items:
            for frame in range(frames):
                base = frame * depth * stride + k * per + plane
                even = source[0, pl.ds(base, depth, stride), :]
                odd = source[1, pl.ds(base, depth, stride), :]
                groups = [even, odd, shifted_columns(even, 1, lanes), shifted_columns(odd, 0, lanes)]
                for image in range(frames):
                    channel = (frame - image) % frames
                    for group in range(4):
                        window[slot, 4 * channel + group, pl.ds(LEAD, depth), pl.ds(image * lanes, lanes)] = groups[group]

    def enter(items):
        pieces = []
        for chunk in range(depth // FIRST):
            for slot, k, plane in items:

                def rows(slot=slot, chunk=chunk):
                    values = window[slot, :, pl.ds(chunk * FIRST, WINDOW), :]
                    return values.astype(BF).reshape(8 * WINDOW, frames * lanes)

                base = row * (1 + chunk * FIRST)
                pieces += first_layer(rows, first_ref.at[k + 1], bias1[k], hidden.at[slot], base, channels)
        return pieces

    def cross(items):
        pieces = []
        for strip in range(depth // 2):
            for slot, k, plane in items:

                def piece(slot=slot, k=k, strip=strip):
                    base = row * (1 + 2 * strip)
                    mid_layer(
                        lambda: hidden[slot, pl.ds(2 * row * strip, 4 * row), :],
                        mid_ref.at[k + 1], bias2[k], deeper.at[slot], base, channels, lanes,
                    )

                pieces.append(piece)
        return pieces

    def leave(items):
        pieces = []
        for chunk in range(depth // CHUNK):
            for slot, k, plane in items:

                def piece(slot=slot, k=k, plane=plane, chunk=chunk):
                    if last_ref.shape[2] == depth * row:
                        slab = deeper[slot, pl.ds(row, depth * row), :]
                    else:
                        slab = deeper[slot, pl.ds(chunk * CHUNK * row, (CHUNK + 2) * row), :]
                    parts = last_layer(slab, last_ref[k + 1], lanes)
                    for half in range(2):
                        for frame in range(frames):
                            base = (frame * depth + chunk * CHUNK) * stride + k * per + plane
                            values = parts[half][:, frame * lanes : (frame + 1) * lanes]
                            result[half, pl.ds(base, CHUNK, stride), :] = values

                pieces.append(piece)
        return pieces

    batches = [
        [(2 * (plane % 2) + k, k, plane) for k in range(2)] for plane in range(per)
    ]
    def mixed(*lists):
        placed = []
        for index, pieces in enumerate(lists):
            placed += [((count + 0.5) / len(pieces), index, count) for count in range(len(pieces))]
        for _, index, count in sorted(placed):
            lists[index][count]()

    fill(batches[0])
    mixed(enter(batches[0]))
    for index in range(per + 1):
        now, coming, going = batches[index : index + 1], batches[index + 1 : index + 2], []
        if index > 0:
            going = batches[index - 1 : index]
        for batch in coming:
            fill(batch)
        mixed(
            [piece for batch in now for piece in cross(batch)],
            [piece for batch in coming for piece in enter(batch)],
            [piece for batch in going for piece in leave(batch)],
        )
    for half in range(2):
        out_ref[:, half * lanes : (half + 1) * lanes] = result[half].astype(BF)


def planes(arrived, first, mid, last, bias, frames, depth):
    rows, n = arrived.shape
    lanes = n // 2
    channels = bias.shape[2]
    per = n // (frames * depth)
    row = 2 * channels
    args = [arrived, first, mid, last, bias]
    return pl.pallas_call(
        functools.partial(planes_kernel, frames, depth, per, channels),
        out_shape=jax.ShapeDtypeStruct((rows, n), BF),
        in_specs=[VM] * len(args),
        out_specs=VM,
        compiler_params=PLANES,
        scratch_shapes=[
            pltpu.VMEM((2, rows, lanes), F32),
            pltpu.VMEM((2, rows, lanes), F32),
            pltpu.VMEM((4, 8, depth + 2 * LEAD, frames * lanes), F32),
            pltpu.VMEM((4, row * (depth + 2), frames * lanes), BF),
            pltpu.VMEM((4, row * (depth + 2), frames * lanes), BF),
        ],
        cost_estimate=cost(2 * 9 * channels * channels * 2 * n * n * 3, 4 * n * n),
        name="planes",
    )(*args)


def volume_kernel(
    channels, mine_ref, other_ref, first_ref, mid_ref, last_ref, bias_ref, states, data, after_ref, out_ref,
    window, hidden, deeper, residual, held, arrival,
):
    copy = pltpu.make_async_copy(states, held, arrival)
    copy.start()
    n = mine_ref.shape[0]
    lanes = n // 2
    row = 2 * channels
    depth = n // 2
    edge = row * (depth + 1)
    zeros = jnp.zeros((8, LEAD, lanes), F32)
    window[:, 0:LEAD, :] = zeros
    window[:, pl.ds(LEAD + n, LEAD), :] = zeros
    for channel, ref in enumerate((mine_ref, other_ref)):
        even = ref[:, :lanes].astype(F32)
        odd = ref[:, lanes:].astype(F32)
        groups = [even, odd, shifted_columns(even, 1, lanes), shifted_columns(odd, 0, lanes)]
        for group in range(4):
            window[4 * channel + group, pl.ds(LEAD, n), :] = groups[group]
    bias1 = jnp.concatenate([bias_ref[0, 0]] * 2, 1)
    bias2 = jnp.concatenate([bias_ref[0, 1]] * 2, 1)

    def seam(ref):
        ref[0:row, 0:lanes] = jnp.zeros((row, lanes), BF)
        ref[pl.ds(edge, row), pl.ds(lanes, lanes)] = jnp.zeros((row, lanes), BF)
        ref[0:row, pl.ds(lanes, lanes)] = ref[pl.ds(edge - row, row), 0:lanes]
        ref[pl.ds(edge, row), 0:lanes] = ref[row : 2 * row, pl.ds(lanes, lanes)]

    def first_chunk(chunk):
        halves = [
            window[:, pl.ds(pl.multiple_of(side * depth + chunk * FIRST, 8), WINDOW), :] for side in range(2)
        ]
        rows = jnp.concatenate(halves, 2).astype(BF).reshape(8 * WINDOW, 2 * lanes)
        base = pl.multiple_of(row * (1 + chunk * FIRST), row)
        for piece in first_layer(lambda: rows, first_ref.at[0], bias1, hidden, base, channels):
            piece()

    def first_step(step, _):
        for inner in range(4):
            first_chunk(step * 4 + inner)
        return 0

    lax.fori_loop(0, depth // (4 * FIRST), first_step, 0)
    seam(hidden)

    def mid_step(step, _):
        for inner in range(16):
            strip = step * 16 + inner
            base = pl.multiple_of(row * (1 + 2 * strip), row)
            mid_layer(
                lambda: hidden[pl.ds(pl.multiple_of(2 * row * strip, row), 4 * row), :],
                mid_ref.at[0], bias2, deeper, base, channels, lanes,
            )
        return 0

    lax.fori_loop(0, depth // 32, mid_step, 0)
    seam(deeper)

    def last_chunk(chunk):
        slab = deeper[pl.ds(pl.multiple_of(chunk * CHUNK * row, row), (CHUNK + 2) * row), :]
        parts = last_layer(slab, last_ref[0], lanes)
        for half in range(2):
            for side in range(2):
                base = pl.multiple_of(side * depth + chunk * CHUNK, CHUNK)
                piece = parts[half][:, side * lanes : (side + 1) * lanes]
                residual[pl.ds(base, CHUNK), pl.ds(half * lanes, lanes)] = piece.astype(BF)

    def last_step(step, _):
        for inner in range(4):
            last_chunk(step * 4 + inner)
        return 0

    lax.fori_loop(0, depth // (4 * CHUNK), last_step, 0)

    copy.wait()
    current = [held[k] for k in range(4)]
    estimates = [data[...], current[1] - nt(residual[...], parity_matrix(n)), current[2], current[3]]
    reflected = [2.0 * estimates[k] - current[k] for k in range(4)]
    average = (reflected[0] + reflected[1] + reflected[2] + reflected[3]) * 0.25
    for k in range(4):
        out_ref[k] = (1.0 - relaxation) * current[k] + relaxation * (2.0 * average - reflected[k])


def volume(mine, other, first, mid, last, bias, current, data, after):
    n = mine.shape[0]
    lanes = n // 2
    channels = bias.shape[2]
    row = 2 * channels
    args = [mine, other, first, mid, last, bias, current, data, after]
    return pl.pallas_call(
        functools.partial(volume_kernel, channels),
        out_shape=jax.ShapeDtypeStruct(current.shape, F32),
        in_specs=[VM] * 6 + [FAR, VM, ANYWHERE],
        out_specs=VM,
        compiler_params=PARAMS,
        scratch_shapes=[
            pltpu.VMEM((8, n + 2 * LEAD, lanes), F32),
            pltpu.VMEM((row * (n // 2 + 2), n), BF),
            pltpu.VMEM((row * (n // 2 + 2), n), BF),
            pltpu.VMEM((n, n), BF),
            pltpu.VMEM(current.shape, F32),
            pltpu.SemaphoreType.DMA,
        ],
        cost_estimate=cost(2 * 9 * channels * channels * n * n * 3, 4 * n * n),
        name="volume",
    )(*args)


def combine_kernel(devices, fast, partial, *refs):
    out, buffer, departure = refs[-3:]
    n = partial.shape[1]
    split = parity_matrix(n)
    if fast:
        per = n // devices
        both = refs[0][...].astype(F32).reshape(devices, 2 * per, n)
        by_x = both[:, :per].reshape(n, n).astype(BF)
        by_y = both[:, per:].reshape(n, n).astype(BF)
    else:
        by_x, by_y = refs[0][...], refs[1][...]
    blocks = 4
    size = n // blocks
    copies = []
    for block in range(blocks):
        rows = slice(block * size, (block + 1) * size)
        res_x = nt(split[rows], by_x)
        res_y = nt(by_y[rows], split)
        common = -relaxation * (res_x + res_y)
        steps = [common, common, common + 2.0 * relaxation * res_x, common + 2.0 * relaxation * res_y]
        for k in range(4):
            buffer[k, rows] = partial[k, rows] + steps[k]
            copy = pltpu.make_async_copy(buffer.at[k, rows], out.at[k, rows], departure.at[block, k])
            copy.start()
            copies.append(copy)
    for copy in copies:
        copy.wait()


def combine(partial, returned, devices):
    n = partial.shape[1]
    per = n // devices
    fast = per % 8 == 0
    if fast:
        parts = [returned]
    else:
        shaped = returned.reshape(devices, 2, per, n)
        parts = [shaped[:, 0].reshape(n, n), shaped[:, 1].reshape(n, n)]
    args = [partial] + parts
    return pl.pallas_call(
        functools.partial(combine_kernel, devices, fast),
        out_shape=jax.ShapeDtypeStruct(partial.shape, F32),
        in_specs=[VM] * len(args),
        out_specs=FAR,
        scratch_shapes=[pltpu.VMEM(partial.shape, F32), pltpu.SemaphoreType.DMA((4, 4))],
        compiler_params=PARAMS,
        cost_estimate=cost(6 * n**3, 40 * n * n),
        name="combine",
    )(*args)


def exchanged(rows, devices):
    n = rows.shape[1]
    blocks = rows.reshape(devices, rows.shape[0] // devices, n)
    blocks = lax.all_to_all(blocks, ("frame", "plane"), split_axis=0, concat_axis=0, tiled=True)
    return blocks.reshape(rows.shape)


def on_device(states, measured, response, kernel_in, bias_in, kernel_mid, bias_mid, kernel_out):
    frames = lax.axis_size("frame")
    depth = lax.axis_size("plane")
    devices = frames * depth
    current = pltpu.with_memory_space_constraint(states[:, 0, 0], pltpu.HBM)
    toward = spread(current, devices)
    mine = own_plane(lax.optimization_barrier((current, toward))[0])
    other = lax.ppermute(mine, "frame", [(f, frames - 1 - f) for f in range(frames)])
    arrived = exchanged(toward, devices)
    data, first, mid, last, inner, bias = prepare(
        current, measured[:, 0], response, kernel_in, bias_in, kernel_mid, bias_mid, kernel_out
    )
    arrived, other = lax.optimization_barrier((arrived, other))
    residual = planes(arrived, first, mid, inner if depth == CHUNK else last, bias, frames, depth)
    returned = exchanged(residual, devices)
    partial = volume(mine, other, first, mid, last, bias, current, data, residual)
    return combine(partial, returned, devices)[:, None, None]


def solution(mesh):
    placed = (
        P(None, "frame", "plane", None, None),
        P("frame", "plane", None, None),
        P(),
        P(),
        P(),
        P(),
        P(),
        P(),
    )
    return jax.shard_map(
        on_device,
        mesh=mesh,
        in_specs=placed,
        out_specs=P(None, "frame", "plane", None, None),
        check_vma=False,
    )
```

```python
import functools
import math

import jax
import jax.numpy as jnp
import numpy as np
from jax import lax
from jax.experimental import pallas as pl
from jax.experimental.pallas import tpu as pltpu
from jax.sharding import PartitionSpec as P

relaxation = 0.8

BF = jnp.bfloat16
F32 = jnp.float32

CHUNK = 16
FIRST = 8
WINDOW = 16
LEAD = 4
PIECE = 4
SPLIT = 1

FIRST_TAP = {(0, 3): 0, (0, 0): 1, (0, 1): 2, (1, 0): 0, (1, 1): 1, (1, 2): 2}
LATER_TAP = {
    (0, 0, 0): 1, (0, 0, 1): 2, (1, 0, 1): 0,
    (0, 1, 0): 0, (0, 1, 1): 1, (1, 1, 0): 2,
}


def fourier_tables(length):
    indices = np.arange(length, dtype=np.int64)
    phase = indices[:, None] * indices[None, :] % length
    angle = phase.astype(np.float32) * np.float32(2.0 * math.pi / length)
    return np.cos(angle).astype(BF), np.sin(angle).astype(BF)


def mm(a, b):
    return jnp.dot(a, b, preferred_element_type=F32)


def nt(a, b):
    return lax.dot_general(a, b, (((1,), (1,)), ((), ())), preferred_element_type=F32)


def tn(a, b):
    return lax.dot_general(a, b, (((0,), (0,)), ((), ())), preferred_element_type=F32)


def iota(shape, axis):
    return lax.broadcasted_iota(jnp.int32, shape, axis)


def parity_matrix(n):
    half = n // 2
    row, col = iota((n, n), 0), iota((n, n), 1)
    natural = jnp.where(col < half, 2 * col, 2 * (col - half) + 1)
    return (row == natural).astype(F32).astype(BF)


VM = pl.BlockSpec(memory_space=pltpu.VMEM)
ANYWHERE = pl.BlockSpec(memory_space=pl.ANY)
FAR = pl.BlockSpec(memory_space=pltpu.HBM)
PARAMS = pltpu.CompilerParams(vmem_limit_bytes=24 << 20)
PLANES = pltpu.CompilerParams(
    vmem_limit_bytes=24 << 20
)


def cost(flops, moved):
    return pl.CostEstimate(flops=flops, bytes_accessed=moved, transcendentals=0)


def spread_kernel(states, out, buffer, parts, arrival, departure):
    n = states.shape[1]
    devices, per = out.shape[0], out.shape[2]
    copies = [pltpu.make_async_copy(states.at[k + 2], buffer.at[k], arrival.at[k]) for k in range(2)]
    for k in (1, 0):
        copies[k].start()
    split = parity_matrix(n)
    leaving = []
    for k in (1, 0):
        copies[k].wait()
        values = buffer[k].astype(BF)
        plane = tn(values, split) if k == 0 else mm(values, split)
        parts[k] = plane.astype(BF).reshape(devices, per, n)
        copy = pltpu.make_async_copy(parts.at[k], out.at[:, k], departure.at[k])
        copy.start()
        leaving.append(copy)
    for copy in leaving:
        copy.wait()


def spread(current, devices):
    n = current.shape[1]
    per = n // devices
    shape = (devices, 2, per, n)
    out = pl.pallas_call(
        spread_kernel,
        out_shape=jax.ShapeDtypeStruct(shape, BF),
        in_specs=[FAR],
        out_specs=FAR,
        scratch_shapes=[
            pltpu.VMEM((2, n, n), F32),
            pltpu.VMEM((2, devices, per, n), BF),
            pltpu.SemaphoreType.DMA((2,)),
            pltpu.SemaphoreType.DMA((2,)),
        ],
        compiler_params=PARAMS,
        cost_estimate=cost(4 * n**3, 12 * n * n),
        name="spread",
    )(current)
    return out.reshape(2 * n, n)


def mine_kernel(states, out_ref, buffer, arrival):
    copy = pltpu.make_async_copy(states.at[1], buffer, arrival)
    copy.start()
    split = parity_matrix(out_ref.shape[0])
    copy.wait()
    out_ref[...] = mm(buffer[...].astype(BF), split).astype(BF)


def own_plane(current):
    n = current.shape[1]
    return pl.pallas_call(
        mine_kernel,
        out_shape=jax.ShapeDtypeStruct((n, n), BF),
        in_specs=[FAR],
        out_specs=VM,
        scratch_shapes=[pltpu.VMEM((n, n), F32), pltpu.SemaphoreType.DMA],
        compiler_params=PARAMS,
        cost_estimate=cost(2 * n**3, 6 * n * n),
        name="own_plane",
    )(current)


def build_first(taps, channels):
    wide = 8 * WINDOW
    lane = iota((channels, wide), 1)
    at_row = lane % WINDOW
    pick_row = iota((6, wide), 0)
    pick_lane = iota((6, wide), 1) // WINDOW
    vectors = {}
    for parity in range(2):
        pick = jnp.zeros((6, wide), F32)
        for group in range(4):
            tap = FIRST_TAP.get((parity, group))
            if tap is not None:
                for source in range(2):
                    hit = (pick_row == 2 * tap + source) & (pick_lane == 4 * source + group)
                    pick = jnp.where(hit, 1.0, pick)
        pick = pick.astype(BF)
        for p in range(3):
            vectors[parity, p] = mm(taps[p], pick)
    pieces = []
    for row in range(FIRST):
        for parity in range(2):
            piece = jnp.zeros((channels, wide), F32)
            for p in range(3):
                piece = jnp.where(at_row == row + LEAD - 1 + p, vectors[parity, p], piece)
            pieces.append(piece.astype(BF))
    return pieces


def build_mid(taps, channels):
    wide = 8 * channels
    block = iota((channels, wide), 1) // channels
    repeat = (iota((channels, wide), 0) == iota((channels, wide), 1) % channels).astype(F32).astype(BF)
    spread_taps = mm(taps, repeat)
    pieces = []
    for row in range(2):
        for parity in range(2):
            for shifted in range(2):
                piece = jnp.zeros((channels, wide), F32)
                for p in range(3):
                    for source in range(2):
                        tap = LATER_TAP.get((shifted, parity, source))
                        if tap is not None:
                            t = 3 * p + tap
                            value = spread_taps[t * channels : (t + 1) * channels]
                            piece = jnp.where(block == 2 * (row + p) + source, value, piece)
                pieces.append(piece.astype(BF))
    return pieces


def build_last(taps, channels):
    wide = (CHUNK + 2) * 2 * channels
    lane = iota((channels, wide), 1)
    at_row = iota((CHUNK, wide), 1) // (2 * channels)
    out_row = iota((CHUNK, wide), 0)
    spread_taps = []
    for source in range(2):
        hit = (lane % channels == iota((channels, wide), 0)) & (lane // channels % 2 == source)
        spread_taps.append(mm(taps, hit.astype(F32).astype(BF)))
    pieces = []
    for shifted in range(2):
        for parity in range(2):
            piece = jnp.zeros((CHUNK, wide), F32)
            for p in range(3):
                value = jnp.zeros((1, wide), F32)
                for source in range(2):
                    tap = LATER_TAP.get((shifted, parity, source))
                    if tap is not None:
                        t = 3 * p + tap
                        value = value + spread_taps[source][t : t + 1]
                piece = jnp.where(at_row == out_row + p, value, piece)
            pieces.append(piece)
    return pieces


def column(row_vector, lanes):
    size = row_vector.shape[1]
    square = iota((size, size), 0) == iota((size, size), 1)
    spread_rows = jnp.where(square, jnp.broadcast_to(row_vector, (size, size)), 0.0)
    return jnp.broadcast_to(jnp.sum(spread_rows, 1, keepdims=True), (size, lanes))


def prepare_kernel(
    states, measured, response, cos_ref, sin_ref, kin, bin_, kmid, bmid, kout,
    data_ref, first_ref, mid_ref, last_ref, inner_ref, bias_ref, w0, arrival,
):
    copy = pltpu.make_async_copy(states.at[0], w0, arrival)
    copy.start()
    n = response.shape[0]
    channels = kmid.shape[2]
    lanes = bias_ref.shape[3]
    cosine, sines = cos_ref[...], sin_ref[...]
    gain = 1.0 / (1.0 + response[...])
    copy.wait()
    source = (measured[0] + w0[...]).astype(BF)
    row_real = mm(source, cosine).astype(BF)
    row_imag = (-mm(source, sines)).astype(BF)
    spec_real = ((mm(cosine, row_real) + mm(sines, row_imag)) * gain).astype(BF)
    spec_imag = ((mm(cosine, row_imag) - mm(sines, row_real)) * gain).astype(BF)
    back_real = (mm(cosine, spec_real) - mm(sines, spec_imag)).astype(BF)
    back_imag = (mm(cosine, spec_imag) + mm(sines, spec_real)).astype(BF)
    data_ref[...] = (mm(back_real, cosine) - mm(back_imag, sines)) * (1.0 / (n * n))
    for which in range(3):
        for index, piece in enumerate(build_first([kin[which, p] for p in range(3)], channels)):
            first_ref[which, pl.ds(index * channels, channels), :] = piece
        for index, piece in enumerate(build_mid(kmid[which], channels)):
            mid_ref[which, pl.ds(index * channels, channels), :] = piece
        for index, piece in enumerate(build_last(kout[which], channels)):
            last_ref[which, pl.ds(index * CHUNK, CHUNK), :] = piece.astype(BF)
            inner = piece[:, 2 * channels : 2 * channels * (CHUNK + 1)]
            inner_ref[which, pl.ds(index * CHUNK, CHUNK), :] = inner.astype(BF)
        bias_ref[which, 0] = column(bin_[pl.ds(which, 1), :], lanes)
        bias_ref[which, 1] = column(bmid[pl.ds(which, 1), :], lanes)


def prepare(current, measured, response, kernel_in, bias_in, kernel_mid, bias_mid, kernel_out):
    n = response.shape[0]
    channels = bias_in.shape[1]
    lanes = n // 2
    cosine, sines = fourier_tables(n)
    kin = kernel_in.reshape(3, 3, 3, channels, 2).transpose(0, 1, 3, 2, 4).reshape(3, 3, channels, 6)
    kmid = kernel_mid[:, 0].reshape(3, 9 * channels, channels)
    bmid = bias_mid[:, 0]
    wide = (CHUNK + 2) * 2 * channels
    shapes = [
        jax.ShapeDtypeStruct((n, n), F32),
        jax.ShapeDtypeStruct((3, FIRST * 2 * channels, 8 * WINDOW), BF),
        jax.ShapeDtypeStruct((3, 8 * channels, 8 * channels), BF),
        jax.ShapeDtypeStruct((3, 4 * CHUNK, wide), BF),
        jax.ShapeDtypeStruct((3, 4 * CHUNK, CHUNK * 2 * channels), BF),
        jax.ShapeDtypeStruct((3, 2, channels, lanes), F32),
    ]
    args = [response, jnp.asarray(cosine), jnp.asarray(sines), kin, bias_in, kmid, bmid, kernel_out]
    return pl.pallas_call(
        prepare_kernel,
        out_shape=shapes,
        in_specs=[FAR] + [VM] * (len(args) + 1),
        out_specs=[VM] * len(shapes),
        scratch_shapes=[pltpu.VMEM((n, n), F32), pltpu.SemaphoreType.DMA],
        compiler_params=PARAMS,
        cost_estimate=cost(40 * n**3, 40 * n * n),
        name="prepare",
    )(current, measured, *args)


def shifted_columns(values, parity, lanes):
    lane = iota((values.shape[0], lanes), 1)
    zero = jnp.zeros((), values.dtype)
    pieces = []
    for start in range(0, values.shape[1], lanes):
        part = values[:, start : start + lanes]
        if parity == 0:
            part = jnp.where(lane == 0, zero, pltpu.roll(part, 1, 1))
        else:
            part = jnp.where(lane == lanes - 1, zero, pltpu.roll(part, lanes - 1, 1))
        pieces.append(part)
    return jnp.concatenate(pieces, 1) if len(pieces) > 1 else pieces[0]


def halve(value):
    return jnp.maximum(value.astype(BF), jnp.zeros((), BF))


def first_layer(window, weights, bias, hidden_ref, base, channels):
    step = PIECE * channels

    def piece(index):
        product = mm(weights[pl.ds(index * step, step), :], window())
        for part in range(step // channels):
            rows = product[part * channels : (part + 1) * channels] + bias
            hidden_ref[pl.ds(base + index * step + part * channels, channels), :] = halve(rows)

    return [functools.partial(piece, index) for index in range(FIRST * 2 * channels // step)]


def mid_layer(slab, weights, bias, out_ref, base, channels, lanes):
    parts = 4 // SPLIT
    step = 2 * parts * channels
    for index in range(SPLIT):
        product = mm(weights[pl.ds(index * step, step), :], slab())
        for part in range(parts):
            kept = product[2 * part * channels : (2 * part + 1) * channels]
            moved = product[(2 * part + 1) * channels : (2 * part + 2) * channels]
            piece = kept + shifted_columns(moved, part % 2 if parts > 1 else index % 2, lanes) + bias
            out_ref[pl.ds(base + (index * parts + part) * channels, channels), :] = halve(piece)


def last_layer(slab, weights, lanes):
    product = mm(weights, slab)
    return [
        product[parity * CHUNK : (parity + 1) * CHUNK]
        + shifted_columns(product[(2 + parity) * CHUNK : (3 + parity) * CHUNK], parity, lanes)
        for parity in range(2)
    ]


def planes_kernel(
    frames, depth, per, channels,
    arrived_ref, first_ref, mid_ref, last_ref, bias_ref, out_ref,
    source, result, window, hidden, deeper,
):
    lanes = arrived_ref.shape[1] // 2
    stride = 2 * per
    row = 2 * channels
    for half in range(2):
        source[half] = arrived_ref[:, half * lanes : (half + 1) * lanes].astype(F32)
    for slot in range(window.shape[0]):
        window[slot, :, 0:LEAD, :] = jnp.zeros((8, LEAD, frames * lanes), F32)
        window[slot, :, pl.ds(LEAD + depth, LEAD), :] = jnp.zeros((8, LEAD, frames * lanes), F32)
    for ref in (hidden, deeper):
        for slot in range(ref.shape[0]):
            ref[slot, 0:row, :] = jnp.zeros((row, frames * lanes), BF)
            ref[slot, pl.ds(row * (depth + 1), row), :] = jnp.zeros((row, frames * lanes), BF)
    bias1 = [jnp.concatenate([bias_ref[k + 1, 0]] * frames, 1) for k in range(2)]
    bias2 = [jnp.concatenate([bias_ref[k + 1, 1]] * frames, 1) for k in range(2)]

    def fill(items):
        for slot, k, plane in items:
            for frame in range(frames):
                base = frame * depth * stride + k * per + plane
                even = source[0, pl.ds(base, depth, stride), :]
                odd = source[1, pl.ds(base, depth, stride), :]
                groups = [even, odd, shifted_columns(even, 1, lanes), shifted_columns(odd, 0, lanes)]
                for image in range(frames):
                    channel = (frame - image) % frames
                    for group in range(4):
                        window[slot, 4 * channel + group, pl.ds(LEAD, depth), pl.ds(image * lanes, lanes)] = groups[group]

    def enter(items):
        pieces = []
        for chunk in range(depth // FIRST):
            for slot, k, plane in items:

                def rows(slot=slot, chunk=chunk):
                    values = window[slot, :, pl.ds(chunk * FIRST, WINDOW), :]
                    return values.astype(BF).reshape(8 * WINDOW, frames * lanes)

                base = row * (1 + chunk * FIRST)
                pieces += first_layer(rows, first_ref.at[k + 1], bias1[k], hidden.at[slot], base, channels)
        return pieces

    def cross(items):
        pieces = []
        for strip in range(depth // 2):
            for slot, k, plane in items:

                def piece(slot=slot, k=k, strip=strip):
                    base = row * (1 + 2 * strip)
                    mid_layer(
                        lambda: hidden[slot, pl.ds(2 * row * strip, 4 * row), :],
                        mid_ref.at[k + 1], bias2[k], deeper.at[slot], base, channels, lanes,
                    )

                pieces.append(piece)
        return pieces

    def leave(items):
        pieces = []
        for chunk in range(depth // CHUNK):
            for slot, k, plane in items:

                def piece(slot=slot, k=k, plane=plane, chunk=chunk):
                    if last_ref.shape[2] == depth * row:
                        slab = deeper[slot, pl.ds(row, depth * row), :]
                    else:
                        slab = deeper[slot, pl.ds(chunk * CHUNK * row, (CHUNK + 2) * row), :]
                    parts = last_layer(slab, last_ref[k + 1], lanes)
                    for half in range(2):
                        for frame in range(frames):
                            base = (frame * depth + chunk * CHUNK) * stride + k * per + plane
                            values = parts[half][:, frame * lanes : (frame + 1) * lanes]
                            result[half, pl.ds(base, CHUNK, stride), :] = values

                pieces.append(piece)
        return pieces

    batches = [
        [(2 * (plane % 2) + k, k, plane) for k in range(2)] for plane in range(per)
    ]
    def mixed(*lists):
        placed = []
        for index, pieces in enumerate(lists):
            placed += [((count + 0.5) / len(pieces), index, count) for count in range(len(pieces))]
        for _, index, count in sorted(placed):
            lists[index][count]()

    fill(batches[0])
    mixed(enter(batches[0]))
    for index in range(per + 1):
        now, coming, going = batches[index : index + 1], batches[index + 1 : index + 2], []
        if index > 0:
            going = batches[index - 1 : index]
        for batch in coming:
            fill(batch)
        mixed(
            [piece for batch in now for piece in cross(batch)],
            [piece for batch in coming for piece in enter(batch)],
            [piece for batch in going for piece in leave(batch)],
        )
    for half in range(2):
        out_ref[:, half * lanes : (half + 1) * lanes] = result[half].astype(BF)


def planes(arrived, first, mid, last, bias, frames, depth):
    rows, n = arrived.shape
    lanes = n // 2
    channels = bias.shape[2]
    per = n // (frames * depth)
    row = 2 * channels
    args = [arrived, first, mid, last, bias]
    return pl.pallas_call(
        functools.partial(planes_kernel, frames, depth, per, channels),
        out_shape=jax.ShapeDtypeStruct((rows, n), BF),
        in_specs=[VM] * len(args),
        out_specs=VM,
        compiler_params=PLANES,
        scratch_shapes=[
            pltpu.VMEM((2, rows, lanes), F32),
            pltpu.VMEM((2, rows, lanes), F32),
            pltpu.VMEM((4, 8, depth + 2 * LEAD, frames * lanes), F32),
            pltpu.VMEM((4, row * (depth + 2), frames * lanes), BF),
            pltpu.VMEM((4, row * (depth + 2), frames * lanes), BF),
        ],
        cost_estimate=cost(2 * 9 * channels * channels * 2 * n * n * 3, 4 * n * n),
        name="planes",
    )(*args)


def volume_kernel(
    channels, mine_ref, other_ref, first_ref, mid_ref, last_ref, bias_ref, states, data, after_ref, out_ref,
    window, hidden, deeper, residual, held, arrival,
):
    copy = pltpu.make_async_copy(states, held, arrival)
    copy.start()
    n = mine_ref.shape[0]
    lanes = n // 2
    row = 2 * channels
    depth = n // 2
    edge = row * (depth + 1)
    zeros = jnp.zeros((8, LEAD, lanes), F32)
    window[:, 0:LEAD, :] = zeros
    window[:, pl.ds(LEAD + n, LEAD), :] = zeros
    for channel, ref in enumerate((mine_ref, other_ref)):
        even = ref[:, :lanes].astype(F32)
        odd = ref[:, lanes:].astype(F32)
        groups = [even, odd, shifted_columns(even, 1, lanes), shifted_columns(odd, 0, lanes)]
        for group in range(4):
            window[4 * channel + group, pl.ds(LEAD, n), :] = groups[group]
    bias1 = jnp.concatenate([bias_ref[0, 0]] * 2, 1)
    bias2 = jnp.concatenate([bias_ref[0, 1]] * 2, 1)

    def seam(ref):
        ref[0:row, 0:lanes] = jnp.zeros((row, lanes), BF)
        ref[pl.ds(edge, row), pl.ds(lanes, lanes)] = jnp.zeros((row, lanes), BF)
        ref[0:row, pl.ds(lanes, lanes)] = ref[pl.ds(edge - row, row), 0:lanes]
        ref[pl.ds(edge, row), 0:lanes] = ref[row : 2 * row, pl.ds(lanes, lanes)]

    def first_chunk(chunk):
        halves = [
            window[:, pl.ds(pl.multiple_of(side * depth + chunk * FIRST, 8), WINDOW), :] for side in range(2)
        ]
        rows = jnp.concatenate(halves, 2).astype(BF).reshape(8 * WINDOW, 2 * lanes)
        base = pl.multiple_of(row * (1 + chunk * FIRST), row)
        for piece in first_layer(lambda: rows, first_ref.at[0], bias1, hidden, base, channels):
            piece()

    def first_step(step, _):
        for inner in range(4):
            first_chunk(step * 4 + inner)
        return 0

    lax.fori_loop(0, depth // (4 * FIRST), first_step, 0)
    seam(hidden)

    def mid_step(step, _):
        for inner in range(16):
            strip = step * 16 + inner
            base = pl.multiple_of(row * (1 + 2 * strip), row)
            mid_layer(
                lambda: hidden[pl.ds(pl.multiple_of(2 * row * strip, row), 4 * row), :],
                mid_ref.at[0], bias2, deeper, base, channels, lanes,
            )
        return 0

    lax.fori_loop(0, depth // 32, mid_step, 0)
    seam(deeper)

    def last_chunk(chunk):
        slab = deeper[pl.ds(pl.multiple_of(chunk * CHUNK * row, row), (CHUNK + 2) * row), :]
        parts = last_layer(slab, last_ref[0], lanes)
        for half in range(2):
            for side in range(2):
                base = pl.multiple_of(side * depth + chunk * CHUNK, CHUNK)
                piece = parts[half][:, side * lanes : (side + 1) * lanes]
                residual[pl.ds(base, CHUNK), pl.ds(half * lanes, lanes)] = piece.astype(BF)

    def last_step(step, _):
        for inner in range(4):
            last_chunk(step * 4 + inner)
        return 0

    lax.fori_loop(0, depth // (4 * CHUNK), last_step, 0)

    copy.wait()
    current = [held[k] for k in range(4)]
    estimates = [data[...], current[1] - nt(residual[...], parity_matrix(n)), current[2], current[3]]
    reflected = [2.0 * estimates[k] - current[k] for k in range(4)]
    average = (reflected[0] + reflected[1] + reflected[2] + reflected[3]) * 0.25
    for k in range(4):
        out_ref[k] = (1.0 - relaxation) * current[k] + relaxation * (2.0 * average - reflected[k])


def volume(mine, other, first, mid, last, bias, current, data, after):
    n = mine.shape[0]
    lanes = n // 2
    channels = bias.shape[2]
    row = 2 * channels
    args = [mine, other, first, mid, last, bias, current, data, after]
    return pl.pallas_call(
        functools.partial(volume_kernel, channels),
        out_shape=jax.ShapeDtypeStruct(current.shape, F32),
        in_specs=[VM] * 6 + [FAR, VM, ANYWHERE],
        out_specs=VM,
        compiler_params=PARAMS,
        scratch_shapes=[
            pltpu.VMEM((8, n + 2 * LEAD, lanes), F32),
            pltpu.VMEM((row * (n // 2 + 2), n), BF),
            pltpu.VMEM((row * (n // 2 + 2), n), BF),
            pltpu.VMEM((n, n), BF),
            pltpu.VMEM(current.shape, F32),
            pltpu.SemaphoreType.DMA,
        ],
        cost_estimate=cost(2 * 9 * channels * channels * n * n * 3, 4 * n * n),
        name="volume",
    )(*args)


def combine_kernel(devices, fast, partial, *refs):
    out, buffer, departure = refs[-3:]
    n = partial.shape[1]
    split = parity_matrix(n)
    if fast:
        per = n // devices
        both = refs[0][...].astype(F32).reshape(devices, 2 * per, n)
        by_x = both[:, :per].reshape(n, n).astype(BF)
        by_y = both[:, per:].reshape(n, n).astype(BF)
    else:
        by_x, by_y = refs[0][...], refs[1][...]
    blocks = 2
    size = n // blocks
    copies = []
    for block in range(blocks):
        rows = slice(block * size, (block + 1) * size)
        res_x = nt(split[rows], by_x)
        res_y = nt(by_y[rows], split)
        common = -relaxation * (res_x + res_y)
        steps = [common, common, common + 2.0 * relaxation * res_x, common + 2.0 * relaxation * res_y]
        for k in range(4):
            buffer[k, rows] = partial[k, rows] + steps[k]
            copy = pltpu.make_async_copy(buffer.at[k, rows], out.at[k, rows], departure.at[block, k])
            copy.start()
            copies.append(copy)
    for copy in copies:
        copy.wait()


def combine(partial, returned, devices):
    n = partial.shape[1]
    per = n // devices
    fast = per % 8 == 0
    if fast:
        parts = [returned]
    else:
        shaped = returned.reshape(devices, 2, per, n)
        parts = [shaped[:, 0].reshape(n, n), shaped[:, 1].reshape(n, n)]
    args = [partial] + parts
    return pl.pallas_call(
        functools.partial(combine_kernel, devices, fast),
        out_shape=jax.ShapeDtypeStruct(partial.shape, F32),
        in_specs=[VM] * len(args),
        out_specs=FAR,
        scratch_shapes=[pltpu.VMEM(partial.shape, F32), pltpu.SemaphoreType.DMA((2, 4))],
        compiler_params=PARAMS,
        cost_estimate=cost(6 * n**3, 40 * n * n),
        name="combine",
    )(*args)


def exchanged(rows, devices):
    n = rows.shape[1]
    blocks = rows.reshape(devices, rows.shape[0] // devices, n)
    blocks = lax.all_to_all(blocks, ("frame", "plane"), split_axis=0, concat_axis=0, tiled=True)
    return blocks.reshape(rows.shape)


def on_device(states, measured, response, kernel_in, bias_in, kernel_mid, bias_mid, kernel_out):
    frames = lax.axis_size("frame")
    depth = lax.axis_size("plane")
    devices = frames * depth
    current = pltpu.with_memory_space_constraint(states[:, 0, 0], pltpu.HBM)
    toward = spread(current, devices)
    mine = own_plane(lax.optimization_barrier((current, toward))[0])
    other = lax.ppermute(mine, "frame", [(f, frames - 1 - f) for f in range(frames)])
    arrived = exchanged(toward, devices)
    data, first, mid, last, inner, bias = prepare(
        current, measured[:, 0], response, kernel_in, bias_in, kernel_mid, bias_mid, kernel_out
    )
    arrived, other = lax.optimization_barrier((arrived, other))
    residual = planes(arrived, first, mid, inner if depth == CHUNK else last, bias, frames, depth)
    returned = exchanged(residual, devices)
    partial = volume(mine, other, first, mid, last, bias, current, data, residual)
    return combine(partial, returned, devices)[:, None, None]


def solution(mesh):
    placed = (
        P(None, "frame", "plane", None, None),
        P("frame", "plane", None, None),
        P(),
        P(),
        P(),
        P(),
        P(),
        P(),
    )
    return jax.shard_map(
        on_device,
        mesh=mesh,
        in_specs=placed,
        out_specs=P(None, "frame", "plane", None, None),
        check_vma=False,
    )
```

```python
import functools
import math

import jax
import jax.numpy as jnp
import numpy as np
from jax import lax
from jax.experimental import pallas as pl
from jax.experimental.pallas import tpu as pltpu
from jax.sharding import PartitionSpec as P

relaxation = 0.8

BF = jnp.bfloat16
F32 = jnp.float32

CHUNK = 16
FIRST = 8
WINDOW = 16
LEAD = 4
PIECE = 4
SPLIT = 1

FIRST_TAP = {(0, 3): 0, (0, 0): 1, (0, 1): 2, (1, 0): 0, (1, 1): 1, (1, 2): 2}
LATER_TAP = {
    (0, 0, 0): 1, (0, 0, 1): 2, (1, 0, 1): 0,
    (0, 1, 0): 0, (0, 1, 1): 1, (1, 1, 0): 2,
}


def fourier_tables(length):
    indices = np.arange(length, dtype=np.int64)
    phase = indices[:, None] * indices[None, :] % length
    angle = phase.astype(np.float32) * np.float32(2.0 * math.pi / length)
    return np.cos(angle).astype(BF), np.sin(angle).astype(BF)


def mm(a, b):
    return jnp.dot(a, b, preferred_element_type=F32)


def nt(a, b):
    return lax.dot_general(a, b, (((1,), (1,)), ((), ())), preferred_element_type=F32)


def tn(a, b):
    return lax.dot_general(a, b, (((0,), (0,)), ((), ())), preferred_element_type=F32)


def iota(shape, axis):
    return lax.broadcasted_iota(jnp.int32, shape, axis)


def parity_matrix(n):
    half = n // 2
    row, col = iota((n, n), 0), iota((n, n), 1)
    natural = jnp.where(col < half, 2 * col, 2 * (col - half) + 1)
    return (row == natural).astype(F32).astype(BF)


VM = pl.BlockSpec(memory_space=pltpu.VMEM)
ANYWHERE = pl.BlockSpec(memory_space=pl.ANY)
FAR = pl.BlockSpec(memory_space=pltpu.HBM)
PARAMS = pltpu.CompilerParams(vmem_limit_bytes=24 << 20)
PLANES = pltpu.CompilerParams(
    vmem_limit_bytes=24 << 20
)


def cost(flops, moved):
    return pl.CostEstimate(flops=flops, bytes_accessed=moved, transcendentals=0)


def spread_kernel(states, out, buffer, parts, arrival, departure):
    n = states.shape[1]
    devices, per = out.shape[0], out.shape[2]
    copies = [pltpu.make_async_copy(states.at[k + 2], buffer.at[k], arrival.at[k]) for k in range(2)]
    for k in (1, 0):
        copies[k].start()
    split = parity_matrix(n)
    leaving = []
    for k in (1, 0):
        copies[k].wait()
        values = buffer[k].astype(BF)
        plane = tn(values, split) if k == 0 else mm(values, split)
        parts[k] = plane.astype(BF).reshape(devices, per, n)
        copy = pltpu.make_async_copy(parts.at[k], out.at[:, k], departure.at[k])
        copy.start()
        leaving.append(copy)
    for copy in leaving:
        copy.wait()


def spread(current, devices):
    n = current.shape[1]
    per = n // devices
    shape = (devices, 2, per, n)
    out = pl.pallas_call(
        spread_kernel,
        out_shape=jax.ShapeDtypeStruct(shape, BF),
        in_specs=[FAR],
        out_specs=FAR,
        scratch_shapes=[
            pltpu.VMEM((2, n, n), F32),
            pltpu.VMEM((2, devices, per, n), BF),
            pltpu.SemaphoreType.DMA((2,)),
            pltpu.SemaphoreType.DMA((2,)),
        ],
        compiler_params=PARAMS,
        cost_estimate=cost(4 * n**3, 12 * n * n),
        name="spread",
    )(current)
    return out.reshape(2 * n, n)


def mine_kernel(states, out_ref, buffer, arrival):
    copy = pltpu.make_async_copy(states.at[1], buffer, arrival)
    copy.start()
    split = parity_matrix(out_ref.shape[0])
    copy.wait()
    out_ref[...] = mm(buffer[...].astype(BF), split).astype(BF)


def own_plane(current):
    n = current.shape[1]
    return pl.pallas_call(
        mine_kernel,
        out_shape=jax.ShapeDtypeStruct((n, n), BF),
        in_specs=[FAR],
        out_specs=VM,
        scratch_shapes=[pltpu.VMEM((n, n), F32), pltpu.SemaphoreType.DMA],
        compiler_params=PARAMS,
        cost_estimate=cost(2 * n**3, 6 * n * n),
        name="own_plane",
    )(current)


def build_first(taps, channels):
    wide = 8 * WINDOW
    lane = iota((channels, wide), 1)
    at_row = lane % WINDOW
    pick_row = iota((6, wide), 0)
    pick_lane = iota((6, wide), 1) // WINDOW
    vectors = {}
    for parity in range(2):
        pick = jnp.zeros((6, wide), F32)
        for group in range(4):
            tap = FIRST_TAP.get((parity, group))
            if tap is not None:
                for source in range(2):
                    hit = (pick_row == 2 * tap + source) & (pick_lane == 4 * source + group)
                    pick = jnp.where(hit, 1.0, pick)
        pick = pick.astype(BF)
        for p in range(3):
            vectors[parity, p] = mm(taps[p], pick)
    pieces = []
    for row in range(FIRST):
        for parity in range(2):
            piece = jnp.zeros((channels, wide), F32)
            for p in range(3):
                piece = jnp.where(at_row == row + LEAD - 1 + p, vectors[parity, p], piece)
            pieces.append(piece.astype(BF))
    return pieces


def build_mid(taps, channels):
    wide = 8 * channels
    block = iota((channels, wide), 1) // channels
    repeat = (iota((channels, wide), 0) == iota((channels, wide), 1) % channels).astype(F32).astype(BF)
    spread_taps = mm(taps, repeat)
    pieces = []
    for row in range(2):
        for parity in range(2):
            for shifted in range(2):
                piece = jnp.zeros((channels, wide), F32)
                for p in range(3):
                    for source in range(2):
                        tap = LATER_TAP.get((shifted, parity, source))
                        if tap is not None:
                            t = 3 * p + tap
                            value = spread_taps[t * channels : (t + 1) * channels]
                            piece = jnp.where(block == 2 * (row + p) + source, value, piece)
                pieces.append(piece.astype(BF))
    return pieces


def build_last(taps, channels):
    wide = (CHUNK + 2) * 2 * channels
    lane = iota((channels, wide), 1)
    at_row = iota((CHUNK, wide), 1) // (2 * channels)
    out_row = iota((CHUNK, wide), 0)
    spread_taps = []
    for source in range(2):
        hit = (lane % channels == iota((channels, wide), 0)) & (lane // channels % 2 == source)
        spread_taps.append(mm(taps, hit.astype(F32).astype(BF)))
    pieces = []
    for shifted in range(2):
        for parity in range(2):
            piece = jnp.zeros((CHUNK, wide), F32)
            for p in range(3):
                value = jnp.zeros((1, wide), F32)
                for source in range(2):
                    tap = LATER_TAP.get((shifted, parity, source))
                    if tap is not None:
                        t = 3 * p + tap
                        value = value + spread_taps[source][t : t + 1]
                piece = jnp.where(at_row == out_row + p, value, piece)
            pieces.append(piece)
    return pieces


def column(row_vector, lanes):
    size = row_vector.shape[1]
    square = iota((size, size), 0) == iota((size, size), 1)
    spread_rows = jnp.where(square, jnp.broadcast_to(row_vector, (size, size)), 0.0)
    return jnp.broadcast_to(jnp.sum(spread_rows, 1, keepdims=True), (size, lanes))


def prepare_kernel(
    states, measured, response, cos_ref, sin_ref, kin, bin_, kmid, bmid, kout,
    data_ref, first_ref, mid_ref, last_ref, inner_ref, bias_ref, w0, arrival,
):
    copy = pltpu.make_async_copy(states.at[0], w0, arrival)
    copy.start()
    n = response.shape[0]
    channels = kmid.shape[2]
    lanes = bias_ref.shape[3]
    cosine, sines = cos_ref[...], sin_ref[...]
    gain = 1.0 / (1.0 + response[...])
    copy.wait()
    source = (measured[0] + w0[...]).astype(BF)
    row_real = mm(source, cosine).astype(BF)
    row_imag = (-mm(source, sines)).astype(BF)
    spec_real = ((mm(cosine, row_real) + mm(sines, row_imag)) * gain).astype(BF)
    spec_imag = ((mm(cosine, row_imag) - mm(sines, row_real)) * gain).astype(BF)
    back_real = (mm(cosine, spec_real) - mm(sines, spec_imag)).astype(BF)
    back_imag = (mm(cosine, spec_imag) + mm(sines, spec_real)).astype(BF)
    data_ref[...] = (mm(back_real, cosine) - mm(back_imag, sines)) * (1.0 / (n * n))
    for which in range(3):
        for index, piece in enumerate(build_first([kin[which, p] for p in range(3)], channels)):
            first_ref[which, pl.ds(index * channels, channels), :] = piece
        for index, piece in enumerate(build_mid(kmid[which], channels)):
            mid_ref[which, pl.ds(index * channels, channels), :] = piece
        for index, piece in enumerate(build_last(kout[which], channels)):
            last_ref[which, pl.ds(index * CHUNK, CHUNK), :] = piece.astype(BF)
            inner = piece[:, 2 * channels : 2 * channels * (CHUNK + 1)]
            inner_ref[which, pl.ds(index * CHUNK, CHUNK), :] = inner.astype(BF)
        bias_ref[which, 0] = column(bin_[pl.ds(which, 1), :], lanes)
        bias_ref[which, 1] = column(bmid[pl.ds(which, 1), :], lanes)


def prepare(current, measured, response, kernel_in, bias_in, kernel_mid, bias_mid, kernel_out):
    n = response.shape[0]
    channels = bias_in.shape[1]
    lanes = n // 2
    cosine, sines = fourier_tables(n)
    kin = kernel_in.reshape(3, 3, 3, channels, 2).transpose(0, 1, 3, 2, 4).reshape(3, 3, channels, 6)
    kmid = kernel_mid[:, 0].reshape(3, 9 * channels, channels)
    bmid = bias_mid[:, 0]
    wide = (CHUNK + 2) * 2 * channels
    shapes = [
        jax.ShapeDtypeStruct((n, n), F32),
        jax.ShapeDtypeStruct((3, FIRST * 2 * channels, 8 * WINDOW), BF),
        jax.ShapeDtypeStruct((3, 8 * channels, 8 * channels), BF),
        jax.ShapeDtypeStruct((3, 4 * CHUNK, wide), BF),
        jax.ShapeDtypeStruct((3, 4 * CHUNK, CHUNK * 2 * channels), BF),
        jax.ShapeDtypeStruct((3, 2, channels, lanes), F32),
    ]
    args = [response, jnp.asarray(cosine), jnp.asarray(sines), kin, bias_in, kmid, bmid, kernel_out]
    return pl.pallas_call(
        prepare_kernel,
        out_shape=shapes,
        in_specs=[FAR] + [VM] * (len(args) + 1),
        out_specs=[VM] * len(shapes),
        scratch_shapes=[pltpu.VMEM((n, n), F32), pltpu.SemaphoreType.DMA],
        compiler_params=PARAMS,
        cost_estimate=cost(40 * n**3, 40 * n * n),
        name="prepare",
    )(current, measured, *args)


def shifted_columns(values, parity, lanes):
    lane = iota((values.shape[0], lanes), 1)
    zero = jnp.zeros((), values.dtype)
    pieces = []
    for start in range(0, values.shape[1], lanes):
        part = values[:, start : start + lanes]
        if parity == 0:
            part = jnp.where(lane == 0, zero, pltpu.roll(part, 1, 1))
        else:
            part = jnp.where(lane == lanes - 1, zero, pltpu.roll(part, lanes - 1, 1))
        pieces.append(part)
    return jnp.concatenate(pieces, 1) if len(pieces) > 1 else pieces[0]


def halve(value):
    return jnp.maximum(value.astype(BF), jnp.zeros((), BF))


def first_layer(window, weights, bias, hidden_ref, base, channels):
    step = PIECE * channels

    def piece(index):
        product = mm(weights[pl.ds(index * step, step), :], window())
        for part in range(step // channels):
            rows = product[part * channels : (part + 1) * channels] + bias
            hidden_ref[pl.ds(base + index * step + part * channels, channels), :] = halve(rows)

    return [functools.partial(piece, index) for index in range(FIRST * 2 * channels // step)]


def mid_layer(slab, weights, bias, out_ref, base, channels, lanes):
    parts = 4 // SPLIT
    step = 2 * parts * channels
    for index in range(SPLIT):
        product = mm(weights[pl.ds(index * step, step), :], slab())
        for part in range(parts):
            kept = product[2 * part * channels : (2 * part + 1) * channels]
            moved = product[(2 * part + 1) * channels : (2 * part + 2) * channels]
            piece = kept + shifted_columns(moved, part % 2 if parts > 1 else index % 2, lanes) + bias
            out_ref[pl.ds(base + (index * parts + part) * channels, channels), :] = halve(piece)


def last_layer(slab, weights, lanes):
    product = mm(weights, slab)
    return [
        product[parity * CHUNK : (parity + 1) * CHUNK]
        + shifted_columns(product[(2 + parity) * CHUNK : (3 + parity) * CHUNK], parity, lanes)
        for parity in range(2)
    ]


def planes_kernel(
    frames, depth, per, channels,
    arrived_ref, first_ref, mid_ref, last_ref, bias_ref, out_ref,
    source, result, window, hidden, deeper, parts, departure,
):
    lanes = arrived_ref.shape[1] // 2
    stride = 2 * per
    leaving = [pltpu.make_async_copy(parts.at[k], out_ref.at[:, k], departure.at[k]) for k in range(2)]
    row = 2 * channels
    for half in range(2):
        source[half] = arrived_ref[:, half * lanes : (half + 1) * lanes].astype(F32)
    for slot in range(window.shape[0]):
        window[slot, :, 0:LEAD, :] = jnp.zeros((8, LEAD, frames * lanes), F32)
        window[slot, :, pl.ds(LEAD + depth, LEAD), :] = jnp.zeros((8, LEAD, frames * lanes), F32)
    for ref in (hidden, deeper):
        for slot in range(ref.shape[0]):
            ref[slot, 0:row, :] = jnp.zeros((row, frames * lanes), BF)
            ref[slot, pl.ds(row * (depth + 1), row), :] = jnp.zeros((row, frames * lanes), BF)
    bias1 = [jnp.concatenate([bias_ref[k + 1, 0]] * frames, 1) for k in range(2)]
    bias2 = [jnp.concatenate([bias_ref[k + 1, 1]] * frames, 1) for k in range(2)]

    def fill(items):
        for slot, k, plane in items:
            for frame in range(frames):
                base = frame * depth * stride + k * per + plane
                even = source[0, pl.ds(base, depth, stride), :]
                odd = source[1, pl.ds(base, depth, stride), :]
                groups = [even, odd, shifted_columns(even, 1, lanes), shifted_columns(odd, 0, lanes)]
                for image in range(frames):
                    channel = (frame - image) % frames
                    for group in range(4):
                        window[slot, 4 * channel + group, pl.ds(LEAD, depth), pl.ds(image * lanes, lanes)] = groups[group]

    def enter(items):
        pieces = []
        for chunk in range(depth // FIRST):
            for slot, k, plane in items:

                def rows(slot=slot, chunk=chunk):
                    values = window[slot, :, pl.ds(chunk * FIRST, WINDOW), :]
                    return values.astype(BF).reshape(8 * WINDOW, frames * lanes)

                base = row * (1 + chunk * FIRST)
                pieces += first_layer(rows, first_ref.at[k + 1], bias1[k], hidden.at[slot], base, channels)
        return pieces

    def cross(items):
        pieces = []
        for strip in range(depth // 2):
            for slot, k, plane in items:

                def piece(slot=slot, k=k, strip=strip):
                    base = row * (1 + 2 * strip)
                    mid_layer(
                        lambda: hidden[slot, pl.ds(2 * row * strip, 4 * row), :],
                        mid_ref.at[k + 1], bias2[k], deeper.at[slot], base, channels, lanes,
                    )

                pieces.append(piece)
        return pieces

    def leave(items):
        pieces = []
        for chunk in range(depth // CHUNK):
            for slot, k, plane in items:

                def piece(slot=slot, k=k, plane=plane, chunk=chunk):
                    if last_ref.shape[2] == depth * row:
                        slab = deeper[slot, pl.ds(row, depth * row), :]
                    else:
                        slab = deeper[slot, pl.ds(chunk * CHUNK * row, (CHUNK + 2) * row), :]
                    pair = last_layer(slab, last_ref[k + 1], lanes)
                    for half in range(2):
                        for frame in range(frames):
                            base = (frame * depth + chunk * CHUNK) * per + plane
                            values = pair[half][:, frame * lanes : (frame + 1) * lanes]
                            result[k, half, pl.ds(base, CHUNK, per), :] = values

                pieces.append(piece)
        return pieces

    def depart(k):
        both = jnp.concatenate([result[k, 0], result[k, 1]], 1).astype(BF)
        parts[k] = both.reshape(parts.shape[1:])
        leaving[k].start()

    batches = []
    for k in range(2):
        for start in range(0, per, 2):
            slot = 2 * (len(batches) % 2)
            batches.append([(slot + side, k, start + side) for side in range(min(2, per - start))])

    def mixed(*lists):
        placed = []
        for index, pieces in enumerate(lists):
            placed += [((count + 0.5) / len(pieces), index, count) for count in range(len(pieces))]
        for _, index, count in sorted(placed):
            lists[index][count]()

    fill(batches[0])
    mixed(enter(batches[0]))
    for index in range(len(batches) + 1):
        now, coming, going = batches[index : index + 1], batches[index + 1 : index + 2], []
        if index > 0:
            going = batches[index - 1 : index]
        for batch in coming:
            fill(batch)
        mixed(
            [piece for batch in now for piece in cross(batch)],
            [piece for batch in coming for piece in enter(batch)],
            [piece for batch in going for piece in leave(batch)],
        )
        if 2 * index == len(batches):
            depart(0)
    depart(1)
    for copy in leaving:
        copy.wait()


def planes(arrived, first, mid, last, bias, frames, depth):
    rows, n = arrived.shape
    lanes = n // 2
    channels = bias.shape[2]
    per = n // (frames * depth)
    row = 2 * channels
    args = [arrived, first, mid, last, bias]
    shape = (frames * depth, 2, per, n)
    out = pl.pallas_call(
        functools.partial(planes_kernel, frames, depth, per, channels),
        out_shape=jax.ShapeDtypeStruct(shape, BF),
        in_specs=[VM] * len(args),
        out_specs=FAR,
        compiler_params=PLANES,
        scratch_shapes=[
            pltpu.VMEM((2, rows, lanes), F32),
            pltpu.VMEM((2, 2, rows // 2, lanes), F32),
            pltpu.VMEM((4, 8, depth + 2 * LEAD, frames * lanes), F32),
            pltpu.VMEM((4, row * (depth + 2), frames * lanes), BF),
            pltpu.VMEM((4, row * (depth + 2), frames * lanes), BF),
            pltpu.VMEM((2, frames * depth, per, n), BF),
            pltpu.SemaphoreType.DMA((2,)),
        ],
        cost_estimate=cost(2 * 9 * channels * channels * 2 * n * n * 3, 4 * n * n),
        name="planes",
    )(*args)
    return out.reshape(rows, n)


def volume_kernel(
    channels, mine_ref, other_ref, first_ref, mid_ref, last_ref, bias_ref, states, data, after_ref, out_ref,
    window, hidden, deeper, residual, held, arrival,
):
    copy = pltpu.make_async_copy(states, held, arrival)
    copy.start()
    n = mine_ref.shape[0]
    lanes = n // 2
    row = 2 * channels
    depth = n // 2
    edge = row * (depth + 1)
    zeros = jnp.zeros((8, LEAD, lanes), F32)
    window[:, 0:LEAD, :] = zeros
    window[:, pl.ds(LEAD + n, LEAD), :] = zeros
    for channel, ref in enumerate((mine_ref, other_ref)):
        even = ref[:, :lanes].astype(F32)
        odd = ref[:, lanes:].astype(F32)
        groups = [even, odd, shifted_columns(even, 1, lanes), shifted_columns(odd, 0, lanes)]
        for group in range(4):
            window[4 * channel + group, pl.ds(LEAD, n), :] = groups[group]
    bias1 = jnp.concatenate([bias_ref[0, 0]] * 2, 1)
    bias2 = jnp.concatenate([bias_ref[0, 1]] * 2, 1)

    def seam(ref):
        ref[0:row, 0:lanes] = jnp.zeros((row, lanes), BF)
        ref[pl.ds(edge, row), pl.ds(lanes, lanes)] = jnp.zeros((row, lanes), BF)
        ref[0:row, pl.ds(lanes, lanes)] = ref[pl.ds(edge - row, row), 0:lanes]
        ref[pl.ds(edge, row), 0:lanes] = ref[row : 2 * row, pl.ds(lanes, lanes)]

    def first_chunk(chunk):
        halves = [
            window[:, pl.ds(pl.multiple_of(side * depth + chunk * FIRST, 8), WINDOW), :] for side in range(2)
        ]
        rows = jnp.concatenate(halves, 2).astype(BF).reshape(8 * WINDOW, 2 * lanes)
        base = pl.multiple_of(row * (1 + chunk * FIRST), row)
        for piece in first_layer(lambda: rows, first_ref.at[0], bias1, hidden, base, channels):
            piece()

    def first_step(step, _):
        for inner in range(4):
            first_chunk(step * 4 + inner)
        return 0

    lax.fori_loop(0, depth // (4 * FIRST), first_step, 0)
    seam(hidden)

    def mid_step(step, _):
        for inner in range(16):
            strip = step * 16 + inner
            base = pl.multiple_of(row * (1 + 2 * strip), row)
            mid_layer(
                lambda: hidden[pl.ds(pl.multiple_of(2 * row * strip, row), 4 * row), :],
                mid_ref.at[0], bias2, deeper, base, channels, lanes,
            )
        return 0

    lax.fori_loop(0, depth // 32, mid_step, 0)
    seam(deeper)

    def last_chunk(chunk):
        slab = deeper[pl.ds(pl.multiple_of(chunk * CHUNK * row, row), (CHUNK + 2) * row), :]
        parts = last_layer(slab, last_ref[0], lanes)
        for half in range(2):
            for side in range(2):
                base = pl.multiple_of(side * depth + chunk * CHUNK, CHUNK)
                piece = parts[half][:, side * lanes : (side + 1) * lanes]
                residual[pl.ds(base, CHUNK), pl.ds(half * lanes, lanes)] = piece.astype(BF)

    def last_step(step, _):
        for inner in range(4):
            last_chunk(step * 4 + inner)
        return 0

    lax.fori_loop(0, depth // (4 * CHUNK), last_step, 0)

    copy.wait()
    current = [held[k] for k in range(4)]
    estimates = [data[...], current[1] - nt(residual[...], parity_matrix(n)), current[2], current[3]]
    reflected = [2.0 * estimates[k] - current[k] for k in range(4)]
    average = (reflected[0] + reflected[1] + reflected[2] + reflected[3]) * 0.25
    for k in range(4):
        out_ref[k] = (1.0 - relaxation) * current[k] + relaxation * (2.0 * average - reflected[k])


def volume(mine, other, first, mid, last, bias, current, data, after):
    n = mine.shape[0]
    lanes = n // 2
    channels = bias.shape[2]
    row = 2 * channels
    args = [mine, other, first, mid, last, bias, current, data, after]
    return pl.pallas_call(
        functools.partial(volume_kernel, channels),
        out_shape=jax.ShapeDtypeStruct(current.shape, F32),
        in_specs=[VM] * 6 + [FAR, VM, ANYWHERE],
        out_specs=VM,
        compiler_params=PARAMS,
        scratch_shapes=[
            pltpu.VMEM((8, n + 2 * LEAD, lanes), F32),
            pltpu.VMEM((row * (n // 2 + 2), n), BF),
            pltpu.VMEM((row * (n // 2 + 2), n), BF),
            pltpu.VMEM((n, n), BF),
            pltpu.VMEM(current.shape, F32),
            pltpu.SemaphoreType.DMA,
        ],
        cost_estimate=cost(2 * 9 * channels * channels * n * n * 3, 4 * n * n),
        name="volume",
    )(*args)


def combine_kernel(devices, fast, partial, *refs):
    out, buffer, departure = refs[-3:]
    n = partial.shape[1]
    split = parity_matrix(n)
    if fast:
        per = n // devices
        both = refs[0][...].astype(F32).reshape(devices, 2 * per, n)
        by_x = both[:, :per].reshape(n, n).astype(BF)
        by_y = both[:, per:].reshape(n, n).astype(BF)
    else:
        by_x, by_y = refs[0][...], refs[1][...]
    blocks = 2
    size = n // blocks
    copies = []
    for block in range(blocks):
        rows = slice(block * size, (block + 1) * size)
        res_x = nt(split[rows], by_x)
        res_y = nt(by_y[rows], split)
        common = -relaxation * (res_x + res_y)
        steps = [common, common, common + 2.0 * relaxation * res_x, common + 2.0 * relaxation * res_y]
        for k in range(4):
            buffer[k, rows] = partial[k, rows] + steps[k]
            copy = pltpu.make_async_copy(buffer.at[k, rows], out.at[k, rows], departure.at[block, k])
            copy.start()
            copies.append(copy)
    for copy in copies:
        copy.wait()


def combine(partial, returned, devices):
    n = partial.shape[1]
    per = n // devices
    fast = per % 8 == 0
    if fast:
        parts = [returned]
    else:
        shaped = returned.reshape(devices, 2, per, n)
        parts = [shaped[:, 0].reshape(n, n), shaped[:, 1].reshape(n, n)]
    args = [partial] + parts
    return pl.pallas_call(
        functools.partial(combine_kernel, devices, fast),
        out_shape=jax.ShapeDtypeStruct(partial.shape, F32),
        in_specs=[VM] * len(args),
        out_specs=FAR,
        scratch_shapes=[pltpu.VMEM(partial.shape, F32), pltpu.SemaphoreType.DMA((2, 4))],
        compiler_params=PARAMS,
        cost_estimate=cost(6 * n**3, 40 * n * n),
        name="combine",
    )(*args)


def exchanged(rows, devices):
    n = rows.shape[1]
    blocks = rows.reshape(devices, rows.shape[0] // devices, n)
    blocks = lax.all_to_all(blocks, ("frame", "plane"), split_axis=0, concat_axis=0, tiled=True)
    return blocks.reshape(rows.shape)


def on_device(states, measured, response, kernel_in, bias_in, kernel_mid, bias_mid, kernel_out):
    frames = lax.axis_size("frame")
    depth = lax.axis_size("plane")
    devices = frames * depth
    current = pltpu.with_memory_space_constraint(states[:, 0, 0], pltpu.HBM)
    toward = spread(current, devices)
    mine = own_plane(lax.optimization_barrier((current, toward))[0])
    other = lax.ppermute(mine, "frame", [(f, frames - 1 - f) for f in range(frames)])
    arrived = exchanged(toward, devices)
    data, first, mid, last, inner, bias = prepare(
        current, measured[:, 0], response, kernel_in, bias_in, kernel_mid, bias_mid, kernel_out
    )
    arrived, other = lax.optimization_barrier((arrived, other))
    residual = planes(arrived, first, mid, inner if depth == CHUNK else last, bias, frames, depth)
    returned = exchanged(residual, devices)
    partial = volume(mine, other, first, mid, last, bias, current, data, residual)
    return combine(partial, returned, devices)[:, None, None]


def solution(mesh):
    placed = (
        P(None, "frame", "plane", None, None),
        P("frame", "plane", None, None),
        P(),
        P(),
        P(),
        P(),
        P(),
        P(),
    )
    return jax.shard_map(
        on_device,
        mesh=mesh,
        in_specs=placed,
        out_specs=P(None, "frame", "plane", None, None),
        check_vma=False,
    )
```
